32 devices in a mesh: ctx: 16 (over z, x, core), rep: 2 (over y).
Axes of the slice: x: 2, y: 2, z: 4, core: 2. Of those that a mesh axis runs over, the one named last changes fastest.
Arguments:
- inputs: bfloat16 [16384, 2880], P(('rep', 'ctx')), parts along dimension 0, may hold values from -64 to 64
- queries: bfloat16 [16384, 2048], P(('rep', 'ctx')), parts along dimension 0, may hold values from -256 to 256
- out_grad: bfloat16 [16384, 2048], P(('rep', 'ctx')), parts along dimension 0, may hold values from -6 to 6
- kv_weight: bfloat16 [1024, 2880], P(('rep', 'ctx')), parts along dimension 0, may hold values from -1 to 1
- sink_logits: float32 [32], replicated, may hold values from -1 to 2
Outputs:
- grad_queries: bfloat16 [16384, 2048], P(('rep', 'ctx')), parts along dimension 0
- grad_input: bfloat16 [16384, 2880], P(('rep', 'ctx')), parts along dimension 0
- grad_weight: float32 [1024, 2880], P(('rep', 'ctx')), parts along dimension 0
The draws below stay inside these ranges and needn't reach their ends.
There are 2 independent parts, one for each index of `rep`. The reference program is written for one: setup_inputs(seed, part) draws one part's arguments, and reference() takes and returns one part's arrays. A program takes and returns all parts, laid end to end along the dimension named above; an argument that names none is the same for every part. Nothing has to cross between parts.
All inputs are finite; a program needn't handle non-finite values.
Results may differ from the reference program's by a relative error of at most 0.011.
Values may be sent and summed in bfloat16 or wider, within the bound.
A program may use at most 128 MiB of HBM per device.

```python
import math
import jax
import jax.numpy as jnp
from jax import lax

D = 2880
HEADS = 32
KV_HEADS = 4
HEAD_DIM = 64
WINDOW = 128
TOK_DEV = 512
SEQ = 8192
GROUP = 8


def kv_table(key):
    raw = jax.random.normal(jax.random.fold_in(key, 7), (2 * KV_HEADS * HEAD_DIM, D), jnp.float32)
    return jnp.clip(raw * (1.0 / math.sqrt(D)), -1.0, 1.0)


def draw_kv_weight(key, part):
    return kv_table(key).astype(jnp.bfloat16)


def draw_inputs(key, part):
    inner = jax.random.fold_in(key, 1)
    base = jnp.clip(jax.random.normal(inner, (SEQ, D), jnp.float32), -6.0, 6.0)
    return base.astype(jnp.bfloat16)


def draw_queries(key, part):
    inner = jax.random.fold_in(key, 2)
    base = jnp.clip(jax.random.normal(inner, (SEQ, HEADS * HEAD_DIM), jnp.float32), -6.0, 6.0)
    return jnp.clip(base, -256.0, 256.0).astype(jnp.bfloat16)


def spiked(entries, key, source, target, parts, factor):
    def block_of(dim):
        return (jnp.arange(entries.shape[dim]) // (entries.shape[dim] // parts)).reshape((-1,) + (1,) * (entries.ndim - 1 - dim))

    first = jax.random.permutation(key, parts)[block_of(target)]
    other_side = (block_of(target) + parts // 2) % parts
    return jnp.where((block_of(source) == first) | (block_of(source) == other_side), factor * entries, entries)


def block_scale(key, extent, shards, low, high):
    def one(dim, parts):
        draws = jax.random.uniform(jax.random.fold_in(jax.random.fold_in(key, 6), dim), (parts,), jnp.float32, low / len(shards), high / len(shards))
        return jnp.repeat(jnp.exp(draws), extent[dim] // parts).reshape((-1,) + (1,) * (len(extent) - dim - 1))

    gain = one(*shards[0])
    for cut in shards[1:]:
        gain = gain * one(*cut)
    return gain


def bell_draw_with(stream_key, shape, scale, limit, cuts, heavy, held_as=jnp.bfloat16):
    entries = scale * jax.random.normal(stream_key, shape, jnp.float32)
    if cuts:
        entries = entries * block_scale(stream_key, shape, cuts, -0.22, 0.18)
    return jnp.clip(spiked(entries, jax.random.fold_in(stream_key, 3), *heavy), -limit, limit).astype(held_as)


def setup_inputs(seed: int = 0, part: int = 0) -> dict:
    key_list = jax.random.split(jax.random.key(seed), 6)
    part_keys = jax.random.split(jax.random.fold_in(key_list[5], part), 6)
    inputs = draw_inputs(jax.random.fold_in(jax.random.fold_in(key_list[5], part), 71), part)
    queries = draw_queries(jax.random.fold_in(jax.random.fold_in(key_list[5], part), 71), part)
    out_grad = bell_draw_with(part_keys[2], (SEQ, HEADS * HEAD_DIM), 1.0, 6.0, ((0, 16),), (0, 1, 16, 2.0))
    kv_weight = draw_kv_weight(jax.random.fold_in(jax.random.fold_in(key_list[5], part), 71), part)
    sink_logits = jnp.clip(jax.random.uniform(key_list[4], (HEADS,), jnp.float32, -1.0, 2.0), -1.0, 2.0)
    return dict(inputs=inputs, queries=queries, out_grad=out_grad, kv_weight=kv_weight, sink_logits=sink_logits)


def pair_tiles(extended, span_rows):
    blocks = extended.reshape((-1, span_rows) + extended.shape[1:])
    return jnp.concatenate([blocks[:-1], blocks[1:]], axis=1)


def fold_tiles(tile_grads, span_rows):
    zero_block = jnp.zeros((1,) + tile_grads.shape[1:2] + tile_grads.shape[2:], tile_grads.dtype)[:, :span_rows]
    lower = jnp.concatenate([tile_grads[:, :span_rows], zero_block], axis=0)
    upper = jnp.concatenate([zero_block, tile_grads[:, span_rows:]], axis=0)
    return lower + upper


def band_grads(query_tiles, grad_tiles, key_tiles, value_tiles, sink_logits, key_first):
    tile_count = query_tiles.shape[0]
    span_rows = query_tiles.shape[1]
    head_groups = query_tiles.shape[2]
    members = query_tiles.shape[3]
    query_wide = query_tiles.astype(jnp.float32)
    grad_wide = grad_tiles.astype(jnp.float32)
    key_wide = key_tiles.astype(jnp.float32)
    value_wide = value_tiles.astype(jnp.float32)
    scores = 0.125 * jnp.einsum("trghd,tcgd->tghrc", query_wide, key_wide)
    row_index = jnp.arange(span_rows, dtype=jnp.int32)[:, None]
    col_index = jnp.arange(2 * span_rows, dtype=jnp.int32)[None, :]
    inside = (col_index > row_index) & (col_index <= row_index + span_rows)
    position = key_first + jnp.arange(tile_count, dtype=jnp.int32)[:, None, None] * span_rows + col_index[None]
    allowed = (inside[None] & (position >= 0))[:, None, None]
    sink_column = sink_logits.reshape(head_groups, members)[None, :, :, None, None]
    masked = jnp.where(allowed, scores, -jnp.inf)
    peak_score = jnp.maximum(jnp.max(masked, axis=-1, keepdims=True), sink_column)
    exp_terms = jnp.where(allowed, jnp.exp(masked - peak_score), 0.0)
    normalizer = jnp.sum(exp_terms, axis=-1, keepdims=True) + jnp.exp(sink_column - peak_score)
    attention = exp_terms / normalizer
    attention_low = lax.optimization_barrier(attention.astype(jnp.bfloat16)).astype(jnp.float32)
    context = jnp.einsum("tghrc,tcgd->trghd", attention_low, value_wide)
    row_delta = jnp.sum(grad_wide * context, axis=-1)
    row_delta = jnp.transpose(row_delta, (0, 2, 3, 1))[..., None]
    grad_attn = jnp.einsum("trghd,tcgd->tghrc", grad_wide, value_wide)
    grad_scores = 0.125 * attention * (grad_attn - row_delta)
    grad_scores = lax.optimization_barrier(grad_scores.astype(jnp.bfloat16)).astype(jnp.float32)
    grad_queries = jnp.einsum("tghrc,tcgd->trghd", grad_scores, key_wide)
    grad_keys = jnp.einsum("tghrc,trghd->tcgd", grad_scores, query_wide)
    grad_values = jnp.einsum("tghrc,trghd->tcgd", attention_low, grad_wide)
    return grad_queries, grad_keys, grad_values


def reference(inputs, queries, out_grad, kv_weight, sink_logits):
    kv_width = KV_HEADS * HEAD_DIM
    projected = jnp.dot(inputs, kv_weight.T, preferred_element_type=jnp.float32).astype(jnp.bfloat16)
    key_rows = projected[:, :kv_width].reshape(SEQ, KV_HEADS, HEAD_DIM)
    value_rows = projected[:, kv_width:].reshape(SEQ, KV_HEADS, HEAD_DIM)
    padding = jnp.zeros((WINDOW, KV_HEADS, HEAD_DIM), jnp.bfloat16)
    key_tiles = pair_tiles(jnp.concatenate([padding, key_rows], axis=0), WINDOW)
    value_tiles = pair_tiles(jnp.concatenate([padding, value_rows], axis=0), WINDOW)
    per_block = TOK_DEV // WINDOW
    block_count = SEQ // TOK_DEV
    query_tiles = queries.reshape(block_count, per_block, WINDOW, KV_HEADS, GROUP, HEAD_DIM)
    grad_tiles = out_grad.reshape(block_count, per_block, WINDOW, KV_HEADS, GROUP, HEAD_DIM)
    key_blocks = key_tiles.reshape((block_count, per_block) + key_tiles.shape[1:])
    value_blocks = value_tiles.reshape((block_count, per_block) + value_tiles.shape[1:])
    key_firsts = jnp.arange(block_count, dtype=jnp.int32) * TOK_DEV - WINDOW

    def one_block(items):
        query_block, grad_block, key_block, value_block, key_first = items
        grad_q, grad_k, grad_v = band_grads(query_block, grad_block, key_block, value_block, sink_logits, key_first)
        return grad_q.astype(jnp.bfloat16), grad_k, grad_v

    grad_q, grad_k, grad_v = lax.map(one_block, (query_tiles, grad_tiles, key_blocks, value_blocks, key_firsts))
    grad_k = grad_k.reshape((SEQ // WINDOW,) + grad_k.shape[2:])
    grad_v = grad_v.reshape((SEQ // WINDOW,) + grad_v.shape[2:])
    key_sum = fold_tiles(grad_k, WINDOW)[1:].reshape(SEQ, kv_width)
    value_sum = fold_tiles(grad_v, WINDOW)[1:].reshape(SEQ, kv_width)
    grad_kv = jnp.concatenate([key_sum, value_sum], axis=1).astype(jnp.bfloat16)
    grad_input = jnp.dot(grad_kv, kv_weight, preferred_element_type=jnp.float32).astype(jnp.bfloat16)
    grad_weight = jnp.dot(grad_kv.T, inputs, preferred_element_type=jnp.float32)
    return grad_q.reshape(SEQ, HEADS * HEAD_DIM), grad_input, grad_weight
```

```python
import functools
import math

import jax
import jax.numpy as jnp
from jax import lax
from jax.experimental import pallas as pl
from jax.experimental.pallas import tpu as pltpu
from jax.sharding import PartitionSpec as P

HEADS = 32
KV_HEADS = 4
HEAD_DIM = 64
WINDOW = 128
GROUP = 8
KV_WIDTH = KV_HEADS * HEAD_DIM
LOG2E = math.log2(math.e)
NEG = -1e30
F32 = jnp.float32
BF16 = jnp.bfloat16


def shifted(block, axis, distance):
    devices = range(lax.axis_size(axis))
    route = [(i - distance, i) for i in devices if i - distance in devices]
    return lax.ppermute(block, axis, route)


def dot(a, b, contract):
    return lax.dot_general(a, b, (contract, ((), ())), preferred_element_type=F32)


def band_kernel(first_ref, sink_ref, q_ref, g_ref, kv_ref, dq_ref, dkv_ref):
    tile = pl.program_id(0)

    @pl.when(tile == 0)
    def _():
        dkv_ref[...] = jnp.zeros_like(dkv_ref)

    start = pl.multiple_of(tile * WINDOW, WINDOW)
    kv = kv_ref[pl.ds(start, 2 * WINDOW), :]
    wide = GROUP * WINDOW
    key_idx = lax.broadcasted_iota(jnp.int32, (WINDOW, wide), 0)
    row_idx = lax.broadcasted_iota(jnp.int32, (WINDOW, wide), 1) % WINDOW
    older = key_idx > row_idx
    bias = jnp.where((first_ref[0] == 0) & (tile == 0), NEG, 0.0).astype(F32)
    dk_parts, dv_parts = [], []
    for g in range(KV_HEADS):
        cols = slice(g * GROUP * HEAD_DIM, (g + 1) * GROUP * HEAD_DIM)
        q_t = q_ref[:, cols].T
        g_t = g_ref[:, cols].T
        pick = [slice(h * HEAD_DIM, (h + 1) * HEAD_DIM) for h in range(GROUP)]
        q_cat = jnp.concatenate([q_t[p] for p in pick], axis=1)
        g_cat = jnp.concatenate([g_t[p] for p in pick], axis=1)
        keys = kv[:, g * HEAD_DIM:(g + 1) * HEAD_DIM]
        values = kv[:, KV_WIDTH + g * HEAD_DIM:KV_WIDTH + (g + 1) * HEAD_DIM]
        s_all = dot(keys, q_cat, ((1,), (0,)))
        s = jnp.where(older, s_all[:WINDOW] + bias, s_all[WINDOW:]) * (0.125 * LOG2E)
        p_all = dot(values, g_cat, ((1,), (0,)))
        grad_attn = jnp.where(older, p_all[:WINDOW], p_all[WINDOW:])
        sink = sink_ref[g:g + 1, :] * LOG2E
        peak = jnp.maximum(jnp.max(s, axis=0, keepdims=True), sink)
        e = jnp.exp2(s - peak)
        norm = jnp.sum(e, axis=0, keepdims=True) + jnp.exp2(sink - peak)
        attn = e * (1.0 / norm)
        low = attn.astype(BF16)
        delta = jnp.sum(low.astype(F32) * grad_attn, axis=0, keepdims=True)
        d_s = (0.125 * attn * (grad_attn - delta)).astype(BF16)
        zero = jnp.zeros_like(low)
        low_all = jnp.concatenate([jnp.where(older, low, zero), jnp.where(older, zero, low)], axis=0)
        ds_all = jnp.concatenate([jnp.where(older, d_s, zero), jnp.where(older, zero, d_s)], axis=0)
        dq_cat = dot(keys.T, ds_all, ((1,), (0,))).astype(BF16)
        dq_t = jnp.concatenate(
            [dq_cat[:, h * WINDOW:(h + 1) * WINDOW] for h in range(GROUP)], axis=0
        )
        dq_ref[:, cols] = dq_t.T
        dk_parts.append(dot(ds_all, q_cat, ((1,), (1,))))
        dv_parts.append(dot(low_all, g_cat, ((1,), (1,))))
    dkv_ref[pl.ds(start, 2 * WINDOW), :] += jnp.concatenate(dk_parts + dv_parts, axis=1)


def band_grads(first, sink_rows, queries, out_grad, kv_ext):
    tok_count, width = queries.shape
    tiles = tok_count // WINDOW
    row_spec = pl.BlockSpec((WINDOW, width), lambda t: (t, 0))
    work = tok_count * 2 * WINDOW * HEADS * HEAD_DIM * 2 * 5
    return pl.pallas_call(
        band_kernel,
        grid=(tiles,),
        in_specs=[
            pl.BlockSpec(memory_space=pltpu.SMEM),
            pl.BlockSpec(sink_rows.shape, lambda t: (0, 0)),
            row_spec,
            row_spec,
            pl.BlockSpec(kv_ext.shape, lambda t: (0, 0)),
        ],
        out_specs=(row_spec, pl.BlockSpec(kv_ext.shape, lambda t: (0, 0))),
        out_shape=(
            jax.ShapeDtypeStruct(queries.shape, BF16),
            jax.ShapeDtypeStruct(kv_ext.shape, F32),
        ),
        compiler_params=pltpu.CompilerParams(
            dimension_semantics=("arbitrary",), vmem_limit_bytes=20 << 20
        ),
        cost_estimate=pl.CostEstimate(
            flops=work, bytes_accessed=6 * tok_count * width, transcendentals=0
        ),
        name="band_grads",
    )(
        first,
        sink_rows,
        queries,
        pltpu.with_memory_space_constraint(out_grad, pltpu.HBM),
        kv_ext,
    )


def peers(lines):
    me = lax.axis_index("ctx").astype(jnp.int32)
    line = lax.div(me, 4)
    side = lax.rem(lax.div(me, 2), 2)
    core = lax.rem(me, 2)

    def at(line_, side_, core_):
        return line_ * 4 + side_ * 2 + core_

    def along(step):
        return lax.rem(line + step + lines, lines)

    return line, side, core, at, along


def greet(lines, targets):
    barrier = pltpu.get_barrier_semaphore()
    _, _, _, before, after = neighbours(lines)

    def signal(target):
        pl.semaphore_signal(
            barrier, inc=1, device_id={"ctx": target}, device_id_type=pl.DeviceIdType.MESH
        )

    for target in targets:
        signal(target)
    signal(before)
    signal(after)
    pl.semaphore_wait(barrier, len(targets) + 2)


def remote(src, dst, send_sem, recv_sem, target):
    return pltpu.make_async_remote_copy(
        src_ref=src,
        dst_ref=dst,
        send_sem=send_sem,
        recv_sem=recv_sem,
        device_id={"ctx": target},
        device_id_type=pl.DeviceIdType.MESH,
    )


def neighbours(lines):
    me = lax.axis_index("ctx").astype(jnp.int32)
    count = 4 * lines
    before, after = lax.rem(me + count - 1, count), lax.rem(me + 1, count)
    return me, me > 0, me < count - 1, before, after


def line_slots(lines):
    return [(0, 0)] + [(d, s) for s in range(1, lines) for d in (1, -1)]


def gather_kernel(
    lines, x_hbm, w_hbm, kv_ref, full_ref, xt_ref, w_ref, ls, zs, zr, xs, xr, cs, cr, hs, hr
):
    w_load = pltpu.make_async_copy(w_hbm, w_ref, ls.at[0])
    x_load = pltpu.make_async_copy(x_hbm, xt_ref, ls.at[1])
    w_load.start()
    x_load.start()
    rows = w_ref.shape[0]
    half = rows // 2
    tok_count = xt_ref.shape[1]
    line, side, core, at, along = peers(lines)
    x_peer = at(line, 1 - side, core)
    c_peer = at(line, side, 1 - core)
    _, has_prev, has_next, _, after = neighbours(lines)
    greet(lines, [x_peer, c_peer] + [at(along(k), side, core) for k in range(1, lines)])

    def inside(step):
        return (line + step >= 0) & (line + step < lines)

    def piece(step, side_, p):
        first = at(along(step), side_, core) * rows + p * half
        return full_ref.at[pl.ds(pl.multiple_of(first, half), half), :]

    def source(slot, p):
        d, s = slot
        return w_ref.at[pl.ds(p * half, half), :] if s == 0 else piece(-d * s, side, p)

    def z_copy(d, s, p):
        i = (0 if d > 0 else 1, s, p)
        return remote(
            source((d, s), p), piece(-d * s, side, p), zs.at[i], zr.at[i], at(along(d), side, core)
        )

    slots = line_slots(lines)

    def x_copy(j, p):
        d, s = slots[j]
        return remote(source(slots[j], p), piece(-d * s, side, p), xs.at[j, p], xr.at[j, p], x_peer)

    def c_near(j, p):
        d, s = slots[j]
        return remote(
            source(slots[j], p), piece(-d * s, side, p), cs.at[j, 0, p], cr.at[j, 0, p], c_peer
        )

    def c_far(j, p):
        d, s = slots[j]
        other = piece(-d * s, 1 - side, p)
        return remote(other, other, cs.at[j, 1, p], cr.at[j, 1, p], c_peer)

    def halo(line_):
        part = pl.ds(pl.multiple_of(line_ * (4 * rows), 4 * rows), 4 * rows)
        return remote(
            kv_ref.at[part, pl.ds(tok_count, WINDOW)],
            kv_ref.at[part, pl.ds(0, WINDOW)],
            hs.at[line_], hr.at[line_], after,
        )

    def valid(j):
        d, s = slots[j]
        return inside(-d * s)

    def land(j):
        d, s = slots[j]

        @pl.when(valid(j))
        def _():
            for p in range(2):
                z_copy(d, s - 1, p).wait_recv()
                if s + 1 < lines:

                    @pl.when(inside(d))
                    def _():
                        z_copy(d, s, p).start()

                x_copy(j, p).start()
                c_near(j, p).start()

    def cross(j):
        @pl.when(valid(j))
        def _():
            for p in range(2):
                x_copy(j, p).wait_recv()
                c_far(j, p).start()

    def finish(j):
        d, s = slots[j]

        @pl.when(valid(j))
        def _():
            for p in range(2):
                c_near(j, p).wait_recv()
                c_far(j, p).wait_recv()
            first = pl.multiple_of(along(-d * s) * (4 * rows), 4 * rows)
            part = full_ref[pl.ds(first, 4 * rows), :]
            chunk = dot(part, xt_ref[...], ((1,), (0,))).astype(BF16)
            kv_ref[pl.ds(first, 4 * rows), WINDOW:] = chunk

            @pl.when(has_next)
            def _():
                halo(along(-d * s)).start()

    w_load.wait()
    for p in range(2):
        for d in (1, -1):

            @pl.when(inside(d))
            def _():
                z_copy(d, 0, p).start()

        x_copy(0, p).start()
    for p in range(2):
        c_near(0, p).start()
    for p in range(2):
        piece(0, side, p)[...] = w_ref[p * half:(p + 1) * half, :]

    @pl.when(jnp.logical_not(has_prev))
    def _():
        kv_ref[:, :WINDOW] = jnp.zeros((kv_ref.shape[0], WINDOW), BF16)

    x_load.wait()
    steps = [[0]] + [[2 * s - 1, 2 * s] for s in range(1, lines)]
    for s in range(1, lines + 2):
        for stage, lag in ((land, 0), (cross, 1), (finish, 2)):
            if 0 <= s - lag < lines:
                for j in steps[s - lag]:
                    stage(j)

    for j, (d, s) in enumerate(slots):

        @pl.when(valid(j))
        def _():
            for p in range(2):
                if s + 1 < lines:
                    for d_ in (1, -1) if s == 0 else (d,):

                        @pl.when(inside(d_))
                        def _():
                            z_copy(d_, s, p).wait_send()

                x_copy(j, p).wait_send()
                c_near(j, p).wait_send()
                c_far(j, p).wait_send()

    for line_ in range(lines):

        @pl.when(has_prev)
        def _():
            halo(line_).wait_recv()

        @pl.when(has_next)
        def _():
            halo(line_).wait_send()


def gather_project(inputs_t, kv_weight, count):
    lines = count // 4
    depth, tok_count = inputs_t.shape
    total = kv_weight.shape[0] * count
    slots = len(line_slots(lines))
    dma = pltpu.SemaphoreType.DMA
    vmem = pl.BlockSpec(memory_space=pltpu.VMEM)
    return pl.pallas_call(
        functools.partial(gather_kernel, lines),
        in_specs=[pl.BlockSpec(memory_space=pltpu.HBM)] * 2,
        out_specs=(vmem, vmem),
        out_shape=(
            jax.ShapeDtypeStruct((total, WINDOW + tok_count), BF16),
            jax.ShapeDtypeStruct((total, depth), BF16),
        ),
        scratch_shapes=[
            pltpu.VMEM(inputs_t.shape, BF16), pltpu.VMEM(kv_weight.shape, BF16), dma((2,)),
            dma((2, lines - 1, 2)), dma((2, lines - 1, 2)), dma((slots, 2)), dma((slots, 2)),
            dma((slots, 2, 2)), dma((slots, 2, 2)), dma((lines,)), dma((lines,)),
        ],
        compiler_params=pltpu.CompilerParams(
            collective_id=0, has_side_effects=True, vmem_limit_bytes=20 << 20
        ),
        name="gather_project",
    )(
        pltpu.with_memory_space_constraint(inputs_t, pltpu.HBM),
        pltpu.with_memory_space_constraint(kv_weight, pltpu.HBM),
    )


def band_scatter_kernel(
    sink_ref, q_ref, g_ref, kv_ref, w_ref, xt_ref, dq_ref, git_ref, gw_ref,
    acc, gkv, h_out, h_in, part, c_buf, c_sum, x_buf, z_out, z_in, t_in,
    hs, hr, cs, cr, xs, xr, zs, zr, tr,
):
    lines = 4
    rows = gw_ref.shape[0]
    half = rows // 2
    tok_count = q_ref.shape[0]
    tiles = tok_count // WINDOW
    wide = GROUP * WINDOW
    group_cols = GROUP * HEAD_DIM
    line, side, core, at, along = peers(lines)
    x_peer = at(line, 1 - side, core)
    c_peer = at(line, side, 1 - core)
    _, has_prev, has_next, before, after = neighbours(lines)
    barrier = pltpu.get_barrier_semaphore()
    partners = [x_peer, c_peer] + [at(along(k), side, core) for k in range(1, lines)]
    for target in partners + [before, after]:
        pl.semaphore_signal(
            barrier, inc=1, device_id={"ctx": target}, device_id_type=pl.DeviceIdType.MESH
        )

    key_idx = lax.broadcasted_iota(jnp.int32, (WINDOW, wide), 0)
    row_idx = lax.broadcasted_iota(jnp.int32, (WINDOW, wide), 1) % WINDOW
    older = key_idx > row_idx
    bias = jnp.where(has_prev, 0.0, NEG).astype(F32)
    groups = [1 - side, side, 3 - side, 2 + side]

    def key_rows(g, values):
        return pl.ds(pl.multiple_of(g * HEAD_DIM + values * KV_WIDTH, HEAD_DIM), HEAD_DIM)

    def band(k, t):
        g = groups[k]
        cols = pl.ds(pl.multiple_of(g * group_cols, group_cols), group_cols)
        here = slice(t * WINDOW, (t + 1) * WINDOW)
        span = slice(t * WINDOW, (t + 2) * WINDOW)
        q_t = q_ref[here, cols].T
        g_t = g_ref[here, cols].T
        pick = [slice(h * HEAD_DIM, (h + 1) * HEAD_DIM) for h in range(GROUP)]
        q_cat = jnp.concatenate([q_t[p] for p in pick], axis=1)
        g_cat = jnp.concatenate([g_t[p] for p in pick], axis=1)
        keys_t = kv_ref[key_rows(g, 0), span]
        values_t = kv_ref[key_rows(g, 1), span]
        s_all = dot(keys_t.T, q_cat, ((1,), (0,)))
        s_old = s_all[:WINDOW] + bias if t == 0 else s_all[:WINDOW]
        s = jnp.where(older, s_old, s_all[WINDOW:]) * (0.125 * LOG2E)
        p_all = dot(values_t.T, g_cat, ((1,), (0,)))
        grad_attn = jnp.where(older, p_all[:WINDOW], p_all[WINDOW:])
        sink = LOG2E * jnp.concatenate(
            [jnp.full((1, WINDOW), sink_ref[g * GROUP + h], F32) for h in range(GROUP)], axis=1
        )
        peak = jnp.maximum(jnp.max(s, axis=0, keepdims=True), sink)
        e = jnp.exp2(s - peak)
        norm = jnp.sum(e, axis=0, keepdims=True) + jnp.exp2(sink - peak)
        attn = e * (1.0 / norm)
        low = attn.astype(BF16)
        delta = jnp.sum(low.astype(F32) * grad_attn, axis=0, keepdims=True)
        d_s = (0.125 * attn * (grad_attn - delta)).astype(BF16)
        zero = jnp.zeros_like(low)
        low_all = jnp.concatenate([jnp.where(older, low, zero), jnp.where(older, zero, low)], axis=0)
        ds_all = jnp.concatenate([jnp.where(older, d_s, zero), jnp.where(older, zero, d_s)], axis=0)
        dq_cat = dot(keys_t, ds_all, ((1,), (0,))).astype(BF16)
        dq_t = jnp.concatenate(
            [dq_cat[:, h * WINDOW:(h + 1) * WINDOW] for h in range(GROUP)], axis=0
        )
        dq_ref[here, cols] = dq_t.T
        for values, (a, b) in enumerate(((q_cat, ds_all), (g_cat, low_all))):
            d_kv = dot(a, b, ((1,), (1,)))
            lo = slice(values * HEAD_DIM, (values + 1) * HEAD_DIM)
            if t == 0:
                acc[k, lo, span] = d_kv
            else:
                acc[k, lo, here] += d_kv[:, :WINDOW]
                acc[k, lo, (t + 1) * WINDOW:(t + 2) * WINDOW] = d_kv[:, WINDOW:]

    def halo(k):
        g = groups[k]
        return remote(h_out.at[g], h_in.at[g], hs.at[g], hr.at[g], before)

    def send_halo(k):
        @pl.when(has_prev)
        def _():
            h_out[groups[k]] = acc[k, :, :WINDOW].astype(BF16)
            halo(k).start()

    def c_copy(k):
        return remote(part.at[k, 1 - core], c_buf.at[k], cs.at[k], cr.at[k], c_peer)

    def finish(k):
        g = groups[k]
        last = slice(tok_count, tok_count + WINDOW)

        @pl.when(has_next)
        def _():
            halo(k).wait_recv()
            acc[k, :, last] += h_in[g].astype(F32)

        grads = acc[k, :, WINDOW:].astype(BF16)
        for values in range(2):
            gkv[key_rows(g, values), :] = grads[values * HEAD_DIM:(values + 1) * HEAD_DIM]
        chunk = dot(grads, xt_ref[...], ((1,), (1,))).astype(BF16)
        for values in range(2):
            for core_ in range(2):
                lo = (2 * values + core_) * rows
                part[k, core_, values] = chunk[lo:lo + rows]
        c_copy(k).start()

    quarters = [(ch, p) for ch in range(2) for p in range(2)]

    def x_copy(a, ch, p):
        span = pl.ds(p * half, half)
        return remote(
            c_sum.at[2 * a, ch, span], x_buf.at[a, ch, span],
            xs.at[a, ch, p], xr.at[a, ch, p], x_peer,
        )

    def join(k):
        c_copy(k).wait_recv()
        for ch in (1, 0) if k == 2 else (0, 1):
            c_sum[k, ch] = (part[k, core, ch].astype(F32) + c_buf[k, ch].astype(F32)).astype(BF16)
            if k % 2 == 0:
                for p in range(2):
                    x_copy(k // 2, ch, p).start()

    def ends(a, ch):
        target = a + 2 * ch
        return target, {0: 3, 3: 0}.get(target), {0: 2, 3: 1}.get(target)

    def z_copy(a, ch, p):
        span = pl.ds(p * half, half)
        target, _, _ = ends(a, ch)
        return remote(
            z_out.at[a, ch, span], z_in.at[line, span],
            zs.at[a, ch, p], zr.at[line, p], at(target, side, core),
        )

    def t_copy(a, ch, p):
        span = pl.ds(p * half, half)
        _, _, middle = ends(a, ch)
        return remote(
            z_out.at[a, ch, span], t_in.at[span], zs.at[a, ch, p], tr.at[p], at(middle, side, core)
        )

    def joined(a, ch, p):
        span = slice(p * half, (p + 1) * half)
        return c_sum[2 * a + 1, ch, span].astype(F32) + x_buf[a, ch, span].astype(F32)

    def join_sides(a, ch, p):
        span = slice(p * half, (p + 1) * half)
        target, leaf, middle = ends(a, ch)
        x_copy(a, ch, p).wait_recv()

        @pl.when(line == target)
        def _():
            gw_ref[span, :] = joined(a, ch, p)

        plain = line != target
        if leaf is not None:
            plain = plain & (line != leaf) & (line != middle)

            @pl.when(line == leaf)
            def _():
                z_out[a, ch, span] = joined(a, ch, p).astype(BF16)
                t_copy(a, ch, p).start()

        @pl.when(plain)
        def _():
            z_out[a, ch, span] = joined(a, ch, p).astype(BF16)
            z_copy(a, ch, p).start()

    def join_lines(a, ch, p):
        span = slice(p * half, (p + 1) * half)
        _, leaf, middle = ends(a, ch)
        if leaf is None:
            return

        @pl.when(line == middle)
        def _():
            t_copy(a, ch, p).wait_recv()
            z_out[a, ch, span] = (joined(a, ch, p) + t_in[span].astype(F32)).astype(BF16)
            z_copy(a, ch, p).start()

    def input_rows(j):
        span = tok_count // 4
        sl = slice(j * span, (j + 1) * span)
        git_ref[:, sl] = dot(gkv[:, sl], w_ref[...], ((0,), (0,))).astype(BF16).T

    band(0, 0)
    band(1, 0)
    pl.semaphore_wait(barrier, len(partners) + 2)
    send_halo(0)
    send_halo(1)
    for t in range(1, tiles):
        band(0, t)
    finish(0)
    band(1, 1)
    join(0)
    for t in range(2, tiles):
        band(1, t)
    finish(1)
    band(2, 0)
    band(3, 0)
    send_halo(2)
    send_halo(3)
    join(1)
    join_sides(0, *quarters[0])
    band(2, 1)
    join_sides(0, *quarters[1])
    band(2, 2)
    join_lines(0, *quarters[0])
    band(2, 3)
    join_sides(0, *quarters[2])
    for t in range(4, tiles):
        band(2, t)
    finish(2)
    join_lines(0, *quarters[1])
    band(3, 1)
    join(2)
    join_sides(0, *quarters[3])
    for t in range(2, tiles):
        band(3, t)
    finish(3)
    input_rows(0)
    join(3)
    later = [quarters[2], quarters[3], quarters[0], quarters[1]]
    for i, q in enumerate(later):
        join_sides(1, *q)
        if i < 3:
            input_rows(i + 1)
        if i:
            join_lines(1, *later[i - 1])
    join_lines(1, *later[3])

    for a in range(2):
        for ch in range(2):
            target, leaf, middle = ends(a, ch)

            @pl.when(line == target)
            def _():
                for source in range(lines):
                    if source not in (target, leaf):
                        for p in range(2):
                            span = slice(p * half, (p + 1) * half)
                            remote(
                                z_out.at[a, ch, pl.ds(p * half, half)],
                                z_in.at[source, pl.ds(p * half, half)],
                                zs.at[a, ch, p], zr.at[source, p], at(source, side, core),
                            ).wait_recv()
                            gw_ref[span, :] += z_in[source, span].astype(F32)

    for k in range(4):
        c_copy(k).wait_send()

        @pl.when(has_prev)
        def _():
            halo(k).wait_send()

    for a in range(2):
        for ch, p in quarters:
            x_copy(a, ch, p).wait_send()

            @pl.when(line != a + 2 * ch)
            def _():
                z_copy(a, ch, p).wait_send()


def band_scatter(sink_logits, queries, out_grad, kv_t, full_weight, inputs_t, count):
    lines = count // 4
    depth, tok_count = inputs_t.shape
    width = full_weight.shape[0]
    rows = width // count
    dma = pltpu.SemaphoreType.DMA
    vmem = pl.BlockSpec(memory_space=pltpu.VMEM)
    low = lambda *shape: pltpu.VMEM(shape, BF16)
    return pl.pallas_call(
        band_scatter_kernel,
        in_specs=[pl.BlockSpec(memory_space=pltpu.SMEM)] + [vmem] * 5,
        out_specs=(vmem, vmem, vmem),
        out_shape=(
            jax.ShapeDtypeStruct(queries.shape, BF16),
            jax.ShapeDtypeStruct((depth, tok_count), BF16),
            jax.ShapeDtypeStruct((rows, depth), F32),
        ),
        scratch_shapes=[
            pltpu.VMEM((KV_HEADS, 2 * HEAD_DIM, WINDOW + tok_count), F32),
            low(width, tok_count),
            low(KV_HEADS, 2 * HEAD_DIM, WINDOW),
            low(KV_HEADS, 2 * HEAD_DIM, WINDOW),
            low(4, 2, 2, rows, depth),
            low(4, 2, rows, depth),
            low(4, 2, rows, depth),
            low(2, 2, rows, depth),
            low(2, 2, rows, depth),
            low(lines, rows, depth),
            low(rows, depth),
            dma((4,)), dma((4,)), dma((4,)), dma((4,)), dma((2, 2, 2)), dma((2, 2, 2)),
            dma((2, 2, 2)), dma((lines, 2)), dma((2,)),
        ],
        compiler_params=pltpu.CompilerParams(
            collective_id=1, has_side_effects=True, vmem_limit_bytes=40 << 20
        ),
        name="band_scatter",
    )(sink_logits, queries, out_grad, kv_t, full_weight, inputs_t)


def shards(inputs, queries, out_grad, kv_weight, sink_logits):
    index = lax.axis_index("ctx")
    count = lax.axis_size("ctx")
    rows = 2 * KV_WIDTH // count
    direct = count == 16 and kv_weight.shape[0] == rows and inputs.shape[0] % (4 * WINDOW) == 0
    if direct:
        inputs_t = inputs.T
        kv_t, full_weight = gather_project(inputs_t, kv_weight, count)
        grad_queries, grad_input_t, grad_weight = band_scatter(
            sink_logits, queries, out_grad, kv_t, full_weight, inputs_t, count
        )
        return (grad_queries, grad_input_t.T, grad_weight)
    full_weight = lax.all_gather(kv_weight, "ctx", axis=0, tiled=True)
    kv_rows = dot(inputs, full_weight, ((1,), (1,))).astype(BF16)
    kv_prev = shifted(kv_rows[-WINDOW:], "ctx", 1)
    kv_ext = jnp.concatenate([kv_prev, kv_rows], axis=0)
    sink_rows = jnp.repeat(sink_logits.reshape(KV_HEADS, GROUP), WINDOW, axis=1)
    grad_queries, grad_ext = band_grads(
        index.astype(jnp.int32).reshape(1), sink_rows, queries, out_grad, kv_ext
    )
    back = shifted(grad_ext[:WINDOW].astype(BF16), "ctx", -1).astype(F32)
    own = grad_ext[WINDOW:]
    grad_kv = jnp.concatenate([own[:-WINDOW], own[-WINDOW:] + back], axis=0).astype(BF16)
    partial = dot(grad_kv, inputs, ((0,), (0,))).astype(BF16)
    grad_weight = lax.psum_scatter(partial, "ctx", scatter_dimension=0, tiled=True).astype(F32)
    grad_input = dot(grad_kv, full_weight, ((1,), (0,))).astype(BF16)
    return (grad_queries, grad_input, grad_weight)


def solution(mesh):
    placed = P(("rep", "ctx"), None)
    return jax.shard_map(
        shards,
        mesh=mesh,
        in_specs=(placed, placed, placed, placed, P()),
        out_specs=(placed, placed, placed),
        check_vma=False,
    )
```

```python
import functools
import math

import jax
import jax.numpy as jnp
from jax import lax
from jax.experimental import pallas as pl
from jax.experimental.pallas import tpu as pltpu
from jax.sharding import PartitionSpec as P

HEADS = 32
KV_HEADS = 4
HEAD_DIM = 64
WINDOW = 128
GROUP = 8
KV_WIDTH = KV_HEADS * HEAD_DIM
LOG2E = math.log2(math.e)
NEG = -1e30
F32 = jnp.float32
BF16 = jnp.bfloat16


def shifted(block, axis, distance):
    devices = range(lax.axis_size(axis))
    route = [(i - distance, i) for i in devices if i - distance in devices]
    return lax.ppermute(block, axis, route)


def dot(a, b, contract):
    return lax.dot_general(a, b, (contract, ((), ())), preferred_element_type=F32)


def band_kernel(first_ref, sink_ref, q_ref, g_ref, kv_ref, dq_ref, dkv_ref):
    tile = pl.program_id(0)

    @pl.when(tile == 0)
    def _():
        dkv_ref[...] = jnp.zeros_like(dkv_ref)

    start = pl.multiple_of(tile * WINDOW, WINDOW)
    kv = kv_ref[pl.ds(start, 2 * WINDOW), :]
    wide = GROUP * WINDOW
    key_idx = lax.broadcasted_iota(jnp.int32, (WINDOW, wide), 0)
    row_idx = lax.broadcasted_iota(jnp.int32, (WINDOW, wide), 1) % WINDOW
    older = key_idx > row_idx
    bias = jnp.where((first_ref[0] == 0) & (tile == 0), NEG, 0.0).astype(F32)
    dk_parts, dv_parts = [], []
    for g in range(KV_HEADS):
        cols = slice(g * GROUP * HEAD_DIM, (g + 1) * GROUP * HEAD_DIM)
        q_t = q_ref[:, cols].T
        g_t = g_ref[:, cols].T
        pick = [slice(h * HEAD_DIM, (h + 1) * HEAD_DIM) for h in range(GROUP)]
        q_cat = jnp.concatenate([q_t[p] for p in pick], axis=1)
        g_cat = jnp.concatenate([g_t[p] for p in pick], axis=1)
        keys = kv[:, g * HEAD_DIM:(g + 1) * HEAD_DIM]
        values = kv[:, KV_WIDTH + g * HEAD_DIM:KV_WIDTH + (g + 1) * HEAD_DIM]
        s_all = dot(keys, q_cat, ((1,), (0,)))
        s = jnp.where(older, s_all[:WINDOW] + bias, s_all[WINDOW:]) * (0.125 * LOG2E)
        p_all = dot(values, g_cat, ((1,), (0,)))
        grad_attn = jnp.where(older, p_all[:WINDOW], p_all[WINDOW:])
        sink = sink_ref[g:g + 1, :] * LOG2E
        peak = jnp.maximum(jnp.max(s, axis=0, keepdims=True), sink)
        e = jnp.exp2(s - peak)
        norm = jnp.sum(e, axis=0, keepdims=True) + jnp.exp2(sink - peak)
        attn = e * (1.0 / norm)
        low = attn.astype(BF16)
        delta = jnp.sum(low.astype(F32) * grad_attn, axis=0, keepdims=True)
        d_s = (0.125 * attn * (grad_attn - delta)).astype(BF16)
        zero = jnp.zeros_like(low)
        low_all = jnp.concatenate([jnp.where(older, low, zero), jnp.where(older, zero, low)], axis=0)
        ds_all = jnp.concatenate([jnp.where(older, d_s, zero), jnp.where(older, zero, d_s)], axis=0)
        dq_cat = dot(keys.T, ds_all, ((1,), (0,))).astype(BF16)
        dq_t = jnp.concatenate(
            [dq_cat[:, h * WINDOW:(h + 1) * WINDOW] for h in range(GROUP)], axis=0
        )
        dq_ref[:, cols] = dq_t.T
        dk_parts.append(dot(ds_all, q_cat, ((1,), (1,))))
        dv_parts.append(dot(low_all, g_cat, ((1,), (1,))))
    dkv_ref[pl.ds(start, 2 * WINDOW), :] += jnp.concatenate(dk_parts + dv_parts, axis=1)


def band_grads(first, sink_rows, queries, out_grad, kv_ext):
    tok_count, width = queries.shape
    tiles = tok_count // WINDOW
    row_spec = pl.BlockSpec((WINDOW, width), lambda t: (t, 0))
    work = tok_count * 2 * WINDOW * HEADS * HEAD_DIM * 2 * 5
    return pl.pallas_call(
        band_kernel,
        grid=(tiles,),
        in_specs=[
            pl.BlockSpec(memory_space=pltpu.SMEM),
            pl.BlockSpec(sink_rows.shape, lambda t: (0, 0)),
            row_spec,
            row_spec,
            pl.BlockSpec(kv_ext.shape, lambda t: (0, 0)),
        ],
        out_specs=(row_spec, pl.BlockSpec(kv_ext.shape, lambda t: (0, 0))),
        out_shape=(
            jax.ShapeDtypeStruct(queries.shape, BF16),
            jax.ShapeDtypeStruct(kv_ext.shape, F32),
        ),
        compiler_params=pltpu.CompilerParams(
            dimension_semantics=("arbitrary",), vmem_limit_bytes=20 << 20
        ),
        cost_estimate=pl.CostEstimate(
            flops=work, bytes_accessed=6 * tok_count * width, transcendentals=0
        ),
        name="band_grads",
    )(
        first,
        sink_rows,
        queries,
        pltpu.with_memory_space_constraint(out_grad, pltpu.HBM),
        kv_ext,
    )


def peers(lines):
    me = lax.axis_index("ctx").astype(jnp.int32)
    line = lax.div(me, 4)
    side = lax.rem(lax.div(me, 2), 2)
    core = lax.rem(me, 2)

    def at(line_, side_, core_):
        return line_ * 4 + side_ * 2 + core_

    def along(step):
        return lax.rem(line + step + lines, lines)

    return line, side, core, at, along


def remote(src, dst, send_sem, recv_sem, target):
    return pltpu.make_async_remote_copy(
        src_ref=src,
        dst_ref=dst,
        send_sem=send_sem,
        recv_sem=recv_sem,
        device_id={"ctx": target},
        device_id_type=pl.DeviceIdType.MESH,
    )


def neighbours(lines):
    me = lax.axis_index("ctx").astype(jnp.int32)
    count = 4 * lines
    before, after = lax.rem(me + count - 1, count), lax.rem(me + 1, count)
    return me, me > 0, me < count - 1, before, after


def line_slots(lines):
    return [(0, 0)] + [(d, s) for s in range(1, lines) for d in (1, -1)]


def fused_kernel(
    sink_hbm, q_hbm, g_hbm, x_hbm, w_hbm, dq_ref, git_ref, gw_ref,
    sink_ref, q_ref, g_ref, xt_ref, own_ref, w_ref, kv_ref,
    acc, gkv, h_out, h_in, part, c_buf, c_sum, x_buf, z_out, z_in, t_in,
    ls, gzs, gzr, gxs, gxr, gcs, gcr, ghs, ghr,
    hs, hr, cs, cr, xs, xr, zs, zr, tr,
):
    lines = 4
    loads = [
        pltpu.make_async_copy(src, dst, ls.at[i])
        for i, (src, dst) in enumerate(
            ((w_hbm, own_ref), (x_hbm, xt_ref), (q_hbm, q_ref), (g_hbm, g_ref), (sink_hbm, sink_ref))
        )
    ]
    for load in loads:
        load.start()
    rows = own_ref.shape[0]
    half = rows // 2
    tok_count = q_ref.shape[0]
    tiles = tok_count // WINDOW
    wide = GROUP * WINDOW
    group_cols = GROUP * HEAD_DIM
    line, side, core, at, along = peers(lines)
    x_peer = at(line, 1 - side, core)
    c_peer = at(line, side, 1 - core)
    _, has_prev, has_next, before, after = neighbours(lines)
    barrier = pltpu.get_barrier_semaphore()
    partners = [x_peer, c_peer] + [at(along(k), side, core) for k in range(1, lines)]
    for target in partners + [before, after]:
        pl.semaphore_signal(
            barrier, inc=1, device_id={"ctx": target}, device_id_type=pl.DeviceIdType.MESH
        )
    pl.semaphore_wait(barrier, len(partners) + 2)

    def inside(step):
        return (line + step >= 0) & (line + step < lines)

    def piece(step, side_, p):
        first = at(along(step), side_, core) * rows + p * half
        return w_ref.at[pl.ds(pl.multiple_of(first, half), half), :]

    def source(slot, p):
        d, s = slot
        return own_ref.at[pl.ds(p * half, half), :] if s == 0 else piece(-d * s, side, p)

    def gz_copy(d, s, p):
        i = (0 if d > 0 else 1, s, p)
        return remote(
            source((d, s), p), piece(-d * s, side, p), gzs.at[i], gzr.at[i],
            at(along(d), side, core),
        )

    slots = line_slots(lines)

    def gx_copy(j, p):
        d, s = slots[j]
        return remote(
            source(slots[j], p), piece(-d * s, side, p), gxs.at[j, p], gxr.at[j, p], x_peer
        )

    def c_near(j, p):
        d, s = slots[j]
        return remote(
            source(slots[j], p), piece(-d * s, side, p), gcs.at[j, 0, p], gcr.at[j, 0, p], c_peer
        )

    def c_far(j, p):
        d, s = slots[j]
        other = piece(-d * s, 1 - side, p)
        return remote(other, other, gcs.at[j, 1, p], gcr.at[j, 1, p], c_peer)

    def kv_halo(line_):
        chunk = pl.ds(pl.multiple_of(line_ * (4 * rows), 4 * rows), 4 * rows)
        return remote(
            kv_ref.at[chunk, pl.ds(tok_count, WINDOW)],
            kv_ref.at[chunk, pl.ds(0, WINDOW)],
            ghs.at[line_], ghr.at[line_], after,
        )

    def valid(j):
        d, s = slots[j]
        return inside(-d * s)

    def land(j):
        d, s = slots[j]

        @pl.when(valid(j))
        def _():
            for p in range(2):
                gz_copy(d, s - 1, p).wait_recv()
                if s + 1 < lines:

                    @pl.when(inside(d))
                    def _():
                        gz_copy(d, s, p).start()

                gx_copy(j, p).start()
                c_near(j, p).start()

    def cross(j):
        @pl.when(valid(j))
        def _():
            for p in range(2):
                gx_copy(j, p).wait_recv()
                c_far(j, p).start()

    def project(j):
        d, s = slots[j]

        @pl.when(valid(j))
        def _():
            for p in range(2):
                c_near(j, p).wait_recv()
                c_far(j, p).wait_recv()
            first = pl.multiple_of(along(-d * s) * (4 * rows), 4 * rows)
            weight = w_ref[pl.ds(first, 4 * rows), :]
            kv_ref[pl.ds(first, 4 * rows), WINDOW:] = dot(
                weight, xt_ref[...], ((1,), (0,))
            ).astype(BF16)

            @pl.when(has_next)
            def _():
                kv_halo(along(-d * s)).start()

    def wait_kv_halo(line_):
        @pl.when(has_prev)
        def _():
            kv_halo(line_).wait_recv()

    key_idx = lax.broadcasted_iota(jnp.int32, (WINDOW, wide), 0)
    row_idx = lax.broadcasted_iota(jnp.int32, (WINDOW, wide), 1) % WINDOW
    older = key_idx > row_idx
    bias = jnp.where(has_prev, 0.0, NEG).astype(F32)
    groups = [1 - side, side, 3 - side, 2 + side]

    def key_rows(g, values):
        return pl.ds(pl.multiple_of(g * HEAD_DIM + values * KV_WIDTH, HEAD_DIM), HEAD_DIM)

    written = set()

    def band(k, t):
        g = groups[k]
        cols = pl.ds(pl.multiple_of(g * group_cols, group_cols), group_cols)
        here = slice(t * WINDOW, (t + 1) * WINDOW)
        span = slice(t * WINDOW, (t + 2) * WINDOW)
        q_t = q_ref[here, cols].T
        g_t = g_ref[here, cols].T
        pick = [slice(h * HEAD_DIM, (h + 1) * HEAD_DIM) for h in range(GROUP)]
        q_cat = jnp.concatenate([q_t[p] for p in pick], axis=1)
        g_cat = jnp.concatenate([g_t[p] for p in pick], axis=1)
        keys_t = kv_ref[key_rows(g, 0), span]
        values_t = kv_ref[key_rows(g, 1), span]
        s_all = dot(keys_t.T, q_cat, ((1,), (0,)))
        s_old = s_all[:WINDOW] + bias if t == 0 else s_all[:WINDOW]
        s = jnp.where(older, s_old, s_all[WINDOW:]) * (0.125 * LOG2E)
        p_all = dot(values_t.T, g_cat, ((1,), (0,)))
        grad_attn = jnp.where(older, p_all[:WINDOW], p_all[WINDOW:])
        sink = LOG2E * jnp.concatenate(
            [jnp.full((1, WINDOW), sink_ref[g * GROUP + h], F32) for h in range(GROUP)], axis=1
        )
        peak = jnp.maximum(jnp.max(s, axis=0, keepdims=True), sink)
        e = jnp.exp2(s - peak)
        norm = jnp.sum(e, axis=0, keepdims=True) + jnp.exp2(sink - peak)
        attn = e * (1.0 / norm)
        low = attn.astype(BF16)
        delta = jnp.sum(low.astype(F32) * grad_attn, axis=0, keepdims=True)
        d_s = (0.125 * attn * (grad_attn - delta)).astype(BF16)
        zero = jnp.zeros_like(low)
        low_all = jnp.concatenate([jnp.where(older, low, zero), jnp.where(older, zero, low)], axis=0)
        ds_all = jnp.concatenate([jnp.where(older, d_s, zero), jnp.where(older, zero, d_s)], axis=0)
        dq_cat = dot(keys_t, ds_all, ((1,), (0,))).astype(BF16)
        dq_t = jnp.concatenate(
            [dq_cat[:, h * WINDOW:(h + 1) * WINDOW] for h in range(GROUP)], axis=0
        )
        dq_ref[here, cols] = dq_t.T
        for values, (a, b) in enumerate(((q_cat, ds_all), (g_cat, low_all))):
            d_kv = dot(a, b, ((1,), (1,)))
            lo = slice(values * HEAD_DIM, (values + 1) * HEAD_DIM)
            for j in range(2):
                block = (k, lo, slice((t + j) * WINDOW, (t + j + 1) * WINDOW))
                grad = d_kv[:, j * WINDOW:(j + 1) * WINDOW]
                if (k, values, t + j) in written:
                    acc[block] += grad
                else:
                    acc[block] = grad
                    written.add((k, values, t + j))

    def halo(k):
        g = groups[k]
        return remote(h_out.at[g], h_in.at[g], hs.at[g], hr.at[g], before)

    def send_halo(k):
        @pl.when(has_prev)
        def _():
            h_out[groups[k]] = acc[k, :, :WINDOW].astype(BF16)
            halo(k).start()

    def c_copy(k):
        return remote(part.at[k, 1 - core], c_buf.at[k], cs.at[k], cr.at[k], c_peer)

    def finish(k):
        g = groups[k]
        last = slice(tok_count, tok_count + WINDOW)

        @pl.when(has_next)
        def _():
            halo(k).wait_recv()
            acc[k, :, last] += h_in[g].astype(F32)

        grads = acc[k, :, WINDOW:].astype(BF16)
        for values in range(2):
            gkv[key_rows(g, values), :] = grads[values * HEAD_DIM:(values + 1) * HEAD_DIM]
        chunk = dot(grads, xt_ref[...], ((1,), (1,))).astype(BF16)
        for values in range(2):
            for core_ in range(2):
                lo = (2 * values + core_) * rows
                part[k, core_, values] = chunk[lo:lo + rows]
        c_copy(k).start()

    quarters = [(ch, p) for ch in range(2) for p in range(2)]

    def x_copy(a, ch, p):
        span = pl.ds(p * half, half)
        return remote(
            c_sum.at[2 * a, ch, span], x_buf.at[a, ch, span],
            xs.at[a, ch, p], xr.at[a, ch, p], x_peer,
        )

    def join(k):
        c_copy(k).wait_recv()
        for ch in (1, 0) if k == 2 else (0, 1):
            c_sum[k, ch] = (part[k, core, ch].astype(F32) + c_buf[k, ch].astype(F32)).astype(BF16)
            if k % 2 == 0:
                for p in range(2):
                    x_copy(k // 2, ch, p).start()

    def ends(a, ch):
        target = a + 2 * ch
        return target, {0: 3, 3: 0}.get(target), {0: 2, 3: 1}.get(target)

    def z_copy(a, ch, p):
        span = pl.ds(p * half, half)
        target, _, _ = ends(a, ch)
        return remote(
            z_out.at[a, ch, span], z_in.at[line, span],
            zs.at[a, ch, p], zr.at[line, p], at(target, side, core),
        )

    def t_copy(a, ch, p):
        span = pl.ds(p * half, half)
        _, _, middle = ends(a, ch)
        return remote(
            z_out.at[a, ch, span], t_in.at[span], zs.at[a, ch, p], tr.at[p], at(middle, side, core)
        )

    def joined(a, ch, p):
        span = slice(p * half, (p + 1) * half)
        return c_sum[2 * a + 1, ch, span].astype(F32) + x_buf[a, ch, span].astype(F32)

    def join_sides(a, ch, p):
        span = slice(p * half, (p + 1) * half)
        target, leaf, middle = ends(a, ch)
        x_copy(a, ch, p).wait_recv()

        @pl.when(line == target)
        def _():
            gw_ref[span, :] = joined(a, ch, p)

        plain = line != target
        if leaf is not None:
            plain = plain & (line != leaf) & (line != middle)

            @pl.when(line == leaf)
            def _():
                z_out[a, ch, span] = joined(a, ch, p).astype(BF16)
                t_copy(a, ch, p).start()

        @pl.when(plain)
        def _():
            z_out[a, ch, span] = joined(a, ch, p).astype(BF16)
            z_copy(a, ch, p).start()

    def join_lines(a, ch, p):
        span = slice(p * half, (p + 1) * half)
        _, leaf, middle = ends(a, ch)
        if leaf is None:
            return

        @pl.when(line == middle)
        def _():
            t_copy(a, ch, p).wait_recv()
            z_out[a, ch, span] = (joined(a, ch, p) + t_in[span].astype(F32)).astype(BF16)
            z_copy(a, ch, p).start()

    def input_rows(j):
        span = tok_count // 4
        sl = slice(j * span, (j + 1) * span)
        git_ref[:, sl] = dot(gkv[:, sl], w_ref[...], ((0,), (0,))).astype(BF16).T

    loads[0].wait()
    for p in range(2):
        for d in (1, -1):

            @pl.when(inside(d))
            def _():
                gz_copy(d, 0, p).start()

        gx_copy(0, p).start()
    for p in range(2):
        c_near(0, p).start()
    for p in range(2):
        piece(0, side, p)[...] = own_ref[p * half:(p + 1) * half, :]

    @pl.when(jnp.logical_not(has_prev))
    def _():
        kv_ref[:, :WINDOW] = jnp.zeros((kv_ref.shape[0], WINDOW), BF16)

    loads[1].wait()
    steps = [[0]] + [[2 * s - 1, 2 * s] for s in range(1, lines)]
    for s in range(1, lines + 2):
        for stage, lag in ((land, 0), (cross, 1), (project, 2)):
            if 0 <= s - lag < lines:
                for j in steps[s - lag]:
                    stage(j)

    for load in loads[2:]:
        load.wait()
    band(0, 1)
    band(0, 2)
    wait_kv_halo(0)
    wait_kv_halo(2)
    band(0, 0)
    band(1, 0)
    send_halo(0)
    send_halo(1)
    for t in range(3, tiles):
        band(0, t)
    finish(0)
    wait_kv_halo(1)
    wait_kv_halo(3)
    band(2, 0)
    band(3, 0)
    send_halo(2)
    send_halo(3)
    join(0)
    for t in range(1, tiles):
        band(2, t)
    finish(2)
    band(1, 1)
    join(2)
    for t in range(2, tiles):
        band(1, t)
    finish(1)
    band(3, 1)
    join(1)
    for q in quarters:
        join_sides(0, *q)
    band(3, 2)
    join_lines(0, *quarters[0])
    band(3, 3)
    join_lines(0, *quarters[1])
    for t in range(4, tiles):
        band(3, t)
    finish(3)
    input_rows(0)
    join(3)
    later = [quarters[2], quarters[3], quarters[0], quarters[1]]
    for i, q in enumerate(later):
        join_sides(1, *q)
        if i < 3:
            input_rows(i + 1)
        if i:
            join_lines(1, *later[i - 1])
    join_lines(1, *later[3])

    for a in range(2):
        for ch in range(2):
            target, leaf, middle = ends(a, ch)

            @pl.when(line == target)
            def _():
                for source in range(lines):
                    if source not in (target, leaf):
                        for p in range(2):
                            span = slice(p * half, (p + 1) * half)
                            remote(
                                z_out.at[a, ch, pl.ds(p * half, half)],
                                z_in.at[source, pl.ds(p * half, half)],
                                zs.at[a, ch, p], zr.at[source, p], at(source, side, core),
                            ).wait_recv()
                            gw_ref[span, :] += z_in[source, span].astype(F32)

    for k in range(4):
        c_copy(k).wait_send()

        @pl.when(has_prev)
        def _():
            halo(k).wait_send()

    for a in range(2):
        for ch, p in quarters:
            x_copy(a, ch, p).wait_send()

            @pl.when(line != a + 2 * ch)
            def _():
                z_copy(a, ch, p).wait_send()

    for j, (d, s) in enumerate(slots):

        @pl.when(valid(j))
        def _():
            for p in range(2):
                if s + 1 < lines:
                    for d_ in (1, -1) if s == 0 else (d,):

                        @pl.when(inside(d_))
                        def _():
                            gz_copy(d_, s, p).wait_send()

                gx_copy(j, p).wait_send()
                c_near(j, p).wait_send()
                c_far(j, p).wait_send()

    for line_ in range(lines):

        @pl.when(has_next)
        def _():
            kv_halo(line_).wait_send()


def fused(sink_logits, queries, out_grad, inputs_t, kv_weight, count):
    lines = count // 4
    depth, tok_count = inputs_t.shape
    rows = kv_weight.shape[0]
    width = rows * count
    slots = len(line_slots(lines))
    dma = pltpu.SemaphoreType.DMA
    vmem = pl.BlockSpec(memory_space=pltpu.VMEM)
    hbm = pl.BlockSpec(memory_space=pltpu.HBM)

    def low(*shape):
        return pltpu.VMEM(shape, BF16)

    operands = [
        pltpu.with_memory_space_constraint(a, pltpu.HBM)
        for a in (sink_logits, queries, out_grad, inputs_t, kv_weight)
    ]
    return pl.pallas_call(
        fused_kernel,
        in_specs=[hbm] * 5,
        out_specs=(vmem, vmem, vmem),
        out_shape=(
            jax.ShapeDtypeStruct(queries.shape, BF16),
            jax.ShapeDtypeStruct((depth, tok_count), BF16),
            jax.ShapeDtypeStruct((rows, depth), F32),
        ),
        scratch_shapes=[
            pltpu.SMEM(sink_logits.shape, F32),
            low(*queries.shape),
            low(*queries.shape),
            low(depth, tok_count),
            low(rows, depth),
            low(width, depth),
            low(width, WINDOW + tok_count),
            pltpu.VMEM((KV_HEADS, 2 * HEAD_DIM, WINDOW + tok_count), F32),
            low(width, tok_count),
            low(KV_HEADS, 2 * HEAD_DIM, WINDOW),
            low(KV_HEADS, 2 * HEAD_DIM, WINDOW),
            low(4, 2, 2, rows, depth),
            low(4, 2, rows, depth),
            low(4, 2, rows, depth),
            low(2, 2, rows, depth),
            low(2, 2, rows, depth),
            low(lines, rows, depth),
            low(rows, depth),
            dma((5,)), dma((2, lines - 1, 2)), dma((2, lines - 1, 2)),
            dma((slots, 2)), dma((slots, 2)), dma((slots, 2, 2)), dma((slots, 2, 2)),
            dma((lines,)), dma((lines,)),
            dma((4,)), dma((4,)), dma((4,)), dma((4,)), dma((2, 2, 2)), dma((2, 2, 2)),
            dma((2, 2, 2)), dma((lines, 2)), dma((2,)),
        ],
        compiler_params=pltpu.CompilerParams(
            collective_id=0, has_side_effects=True, vmem_limit_bytes=48 << 20
        ),
        name="fused",
    )(*operands)


def store_kernel(dq_ref, git_ref, gw_ref, dq_hbm, git_hbm, gw_hbm, sems):
    copies = []
    for src, dst, cuts in ((git_ref, git_hbm, 5), (dq_ref, dq_hbm, 4), (gw_ref, gw_hbm, 1)):
        step = src.shape[0] // cuts
        for i in range(cuts):
            span = pl.ds(i * step, step)
            copies.append(pltpu.make_async_copy(src.at[span], dst.at[span], sems.at[len(copies)]))
    for copy in copies:
        copy.start()
    for copy in copies:
        copy.wait()


def store(*arrays):
    return pl.pallas_call(
        store_kernel,
        in_specs=[pl.BlockSpec(memory_space=pltpu.VMEM)] * 3,
        out_specs=[pl.BlockSpec(memory_space=pltpu.HBM)] * 3,
        out_shape=[jax.ShapeDtypeStruct(a.shape, a.dtype) for a in arrays],
        scratch_shapes=[pltpu.SemaphoreType.DMA((10,))],
        compiler_params=pltpu.CompilerParams(vmem_limit_bytes=8 << 20),
        name="store",
    )(*arrays)


def shards(inputs, queries, out_grad, kv_weight, sink_logits):
    index = lax.axis_index("ctx")
    count = lax.axis_size("ctx")
    rows = 2 * KV_WIDTH // count
    direct = count == 16 and kv_weight.shape[0] == rows and inputs.shape[0] % (4 * WINDOW) == 0
    if direct:
        inputs_t = inputs.T
        grad_queries, grad_input_t, grad_weight = fused(
            sink_logits, queries, out_grad, inputs_t, kv_weight, count
        )
        grad_queries, grad_input_t, grad_weight = store(grad_queries, grad_input_t, grad_weight)
        return (grad_queries, grad_input_t.T, grad_weight)
    full_weight = lax.all_gather(kv_weight, "ctx", axis=0, tiled=True)
    kv_rows = dot(inputs, full_weight, ((1,), (1,))).astype(BF16)
    kv_prev = shifted(kv_rows[-WINDOW:], "ctx", 1)
    kv_ext = jnp.concatenate([kv_prev, kv_rows], axis=0)
    sink_rows = jnp.repeat(sink_logits.reshape(KV_HEADS, GROUP), WINDOW, axis=1)
    grad_queries, grad_ext = band_grads(
        index.astype(jnp.int32).reshape(1), sink_rows, queries, out_grad, kv_ext
    )
    back = shifted(grad_ext[:WINDOW].astype(BF16), "ctx", -1).astype(F32)
    own = grad_ext[WINDOW:]
    grad_kv = jnp.concatenate([own[:-WINDOW], own[-WINDOW:] + back], axis=0).astype(BF16)
    partial = dot(grad_kv, inputs, ((0,), (0,))).astype(BF16)
    grad_weight = lax.psum_scatter(partial, "ctx", scatter_dimension=0, tiled=True).astype(F32)
    grad_input = dot(grad_kv, full_weight, ((1,), (0,))).astype(BF16)
    return (grad_queries, grad_input, grad_weight)


def solution(mesh):
    placed = P(("rep", "ctx"), None)
    return jax.shard_map(
        shards,
        mesh=mesh,
        in_specs=(placed, placed, placed, placed, P()),
        out_specs=(placed, placed, placed),
        check_vma=False,
    )
```

```python
import functools
import math

import jax
import jax.numpy as jnp
from jax import lax
from jax.experimental import pallas as pl
from jax.experimental.pallas import tpu as pltpu
from jax.sharding import PartitionSpec as P

HEADS = 32
KV_HEADS = 4
HEAD_DIM = 64
WINDOW = 128
GROUP = 8
KV_WIDTH = KV_HEADS * HEAD_DIM
LOG2E = math.log2(math.e)
NEG = -1e30
F32 = jnp.float32
BF16 = jnp.bfloat16


def shifted(block, axis, distance):
    devices = range(lax.axis_size(axis))
    route = [(i - distance, i) for i in devices if i - distance in devices]
    return lax.ppermute(block, axis, route)


def dot(a, b, contract):
    return lax.dot_general(a, b, (contract, ((), ())), preferred_element_type=F32)


def band_kernel(first_ref, sink_ref, q_ref, g_ref, kv_ref, dq_ref, dkv_ref):
    tile = pl.program_id(0)

    @pl.when(tile == 0)
    def _():
        dkv_ref[...] = jnp.zeros_like(dkv_ref)

    start = pl.multiple_of(tile * WINDOW, WINDOW)
    kv = kv_ref[pl.ds(start, 2 * WINDOW), :]
    wide = GROUP * WINDOW
    key_idx = lax.broadcasted_iota(jnp.int32, (WINDOW, wide), 0)
    row_idx = lax.broadcasted_iota(jnp.int32, (WINDOW, wide), 1) % WINDOW
    older = key_idx > row_idx
    bias = jnp.where((first_ref[0] == 0) & (tile == 0), NEG, 0.0).astype(F32)
    dk_parts, dv_parts = [], []
    for g in range(KV_HEADS):
        cols = slice(g * GROUP * HEAD_DIM, (g + 1) * GROUP * HEAD_DIM)
        q_t = q_ref[:, cols].T
        g_t = g_ref[:, cols].T
        pick = [slice(h * HEAD_DIM, (h + 1) * HEAD_DIM) for h in range(GROUP)]
        q_cat = jnp.concatenate([q_t[p] for p in pick], axis=1)
        g_cat = jnp.concatenate([g_t[p] for p in pick], axis=1)
        keys = kv[:, g * HEAD_DIM:(g + 1) * HEAD_DIM]
        values = kv[:, KV_WIDTH + g * HEAD_DIM:KV_WIDTH + (g + 1) * HEAD_DIM]
        s_all = dot(keys, q_cat, ((1,), (0,)))
        s = jnp.where(older, s_all[:WINDOW] + bias, s_all[WINDOW:]) * (0.125 * LOG2E)
        p_all = dot(values, g_cat, ((1,), (0,)))
        grad_attn = jnp.where(older, p_all[:WINDOW], p_all[WINDOW:])
        sink = sink_ref[g:g + 1, :] * LOG2E
        peak = jnp.maximum(jnp.max(s, axis=0, keepdims=True), sink)
        e = jnp.exp2(s - peak)
        norm = jnp.sum(e, axis=0, keepdims=True) + jnp.exp2(sink - peak)
        attn = e * (1.0 / norm)
        low = attn.astype(BF16)
        delta = jnp.sum(low.astype(F32) * grad_attn, axis=0, keepdims=True)
        d_s = (0.125 * attn * (grad_attn - delta)).astype(BF16)
        zero = jnp.zeros_like(low)
        low_all = jnp.concatenate([jnp.where(older, low, zero), jnp.where(older, zero, low)], axis=0)
        ds_all = jnp.concatenate([jnp.where(older, d_s, zero), jnp.where(older, zero, d_s)], axis=0)
        dq_cat = dot(keys.T, ds_all, ((1,), (0,))).astype(BF16)
        dq_t = jnp.concatenate(
            [dq_cat[:, h * WINDOW:(h + 1) * WINDOW] for h in range(GROUP)], axis=0
        )
        dq_ref[:, cols] = dq_t.T
        dk_parts.append(dot(ds_all, q_cat, ((1,), (1,))))
        dv_parts.append(dot(low_all, g_cat, ((1,), (1,))))
    dkv_ref[pl.ds(start, 2 * WINDOW), :] += jnp.concatenate(dk_parts + dv_parts, axis=1)


def band_grads(first, sink_rows, queries, out_grad, kv_ext):
    tok_count, width = queries.shape
    tiles = tok_count // WINDOW
    row_spec = pl.BlockSpec((WINDOW, width), lambda t: (t, 0))
    work = tok_count * 2 * WINDOW * HEADS * HEAD_DIM * 2 * 5
    return pl.pallas_call(
        band_kernel,
        grid=(tiles,),
        in_specs=[
            pl.BlockSpec(memory_space=pltpu.SMEM),
            pl.BlockSpec(sink_rows.shape, lambda t: (0, 0)),
            row_spec,
            row_spec,
            pl.BlockSpec(kv_ext.shape, lambda t: (0, 0)),
        ],
        out_specs=(row_spec, pl.BlockSpec(kv_ext.shape, lambda t: (0, 0))),
        out_shape=(
            jax.ShapeDtypeStruct(queries.shape, BF16),
            jax.ShapeDtypeStruct(kv_ext.shape, F32),
        ),
        compiler_params=pltpu.CompilerParams(
            dimension_semantics=("arbitrary",), vmem_limit_bytes=20 << 20
        ),
        cost_estimate=pl.CostEstimate(
            flops=work, bytes_accessed=6 * tok_count * width, transcendentals=0
        ),
        name="band_grads",
    )(
        first,
        sink_rows,
        queries,
        pltpu.with_memory_space_constraint(out_grad, pltpu.HBM),
        kv_ext,
    )


def peers(lines):
    me = lax.axis_index("ctx").astype(jnp.int32)
    line = lax.div(me, 4)
    side = lax.rem(lax.div(me, 2), 2)
    core = lax.rem(me, 2)

    def at(line_, side_, core_):
        return line_ * 4 + side_ * 2 + core_

    def along(step):
        return lax.rem(line + step + lines, lines)

    return line, side, core, at, along


def remote(src, dst, send_sem, recv_sem, target):
    return pltpu.make_async_remote_copy(
        src_ref=src,
        dst_ref=dst,
        send_sem=send_sem,
        recv_sem=recv_sem,
        device_id={"ctx": target},
        device_id_type=pl.DeviceIdType.MESH,
    )


def neighbours(lines):
    me = lax.axis_index("ctx").astype(jnp.int32)
    count = 4 * lines
    before, after = lax.rem(me + count - 1, count), lax.rem(me + 1, count)
    return me, me > 0, me < count - 1, before, after


def line_slots(lines):
    return [(0, 0)] + [(d, s) for s in range(1, lines) for d in (1, -1)]


def fused_kernel(
    sink_hbm, q_hbm, g_hbm, x_hbm, w_hbm, dq_ref, git_ref, gw_ref,
    sink_ref, q_ref, g_ref, xt_ref, x_ref, own_ref, w_ref, kv_ref,
    acc, gkv, h_out, h_in, part, c_buf, c_sum, x_buf, z_out, z_in, t_in,
    ls, gzs, gzr, gxs, gxr, gcs, gcr, ghs, ghr,
    hs, hr, cs, cr, xs, xr, zs, zr, tr,
):
    lines = 4
    loads = [
        pltpu.make_async_copy(src, dst, ls.at[i])
        for i, (src, dst) in enumerate(
            ((w_hbm, own_ref), (x_hbm, xt_ref), (q_hbm, q_ref), (g_hbm, g_ref), (sink_hbm, sink_ref))
        )
    ]
    for load in loads:
        load.start()
    rows = own_ref.shape[0]
    half = rows // 2
    tok_count = q_ref.shape[0]
    tiles = tok_count // WINDOW
    wide = GROUP * WINDOW
    group_cols = GROUP * HEAD_DIM
    line, side, core, at, along = peers(lines)
    x_peer = at(line, 1 - side, core)
    c_peer = at(line, side, 1 - core)
    _, has_prev, has_next, before, after = neighbours(lines)
    barrier = pltpu.get_barrier_semaphore()
    partners = [x_peer, c_peer] + [at(along(k), side, core) for k in range(1, lines)]
    for target in partners + [before, after]:
        pl.semaphore_signal(
            barrier, inc=1, device_id={"ctx": target}, device_id_type=pl.DeviceIdType.MESH
        )
    pl.semaphore_wait(barrier, len(partners) + 2)

    def inside(step):
        return (line + step >= 0) & (line + step < lines)

    def piece(step, side_, p):
        first = at(along(step), side_, core) * rows + p * half
        return w_ref.at[pl.ds(pl.multiple_of(first, half), half), :]

    def source(slot, p):
        d, s = slot
        return own_ref.at[pl.ds(p * half, half), :] if s == 0 else piece(-d * s, side, p)

    def gz_copy(d, s, p):
        i = (0 if d > 0 else 1, s, p)
        return remote(
            source((d, s), p), piece(-d * s, side, p), gzs.at[i], gzr.at[i],
            at(along(d), side, core),
        )

    slots = line_slots(lines)

    def gx_copy(j, p):
        d, s = slots[j]
        return remote(
            source(slots[j], p), piece(-d * s, side, p), gxs.at[j, p], gxr.at[j, p], x_peer
        )

    def c_near(j, p):
        d, s = slots[j]
        return remote(
            source(slots[j], p), piece(-d * s, side, p), gcs.at[j, 0, p], gcr.at[j, 0, p], c_peer
        )

    def c_far(j, p):
        d, s = slots[j]
        other = piece(-d * s, 1 - side, p)
        return remote(other, other, gcs.at[j, 1, p], gcr.at[j, 1, p], c_peer)

    def kv_halo(line_):
        chunk = pl.ds(pl.multiple_of(line_ * (4 * rows), 4 * rows), 4 * rows)
        return remote(
            kv_ref.at[chunk, pl.ds(tok_count, WINDOW)],
            kv_ref.at[chunk, pl.ds(0, WINDOW)],
            ghs.at[line_], ghr.at[line_], after,
        )

    def valid(j):
        d, s = slots[j]
        return inside(-d * s)

    def land(j):
        d, s = slots[j]

        @pl.when(valid(j))
        def _():
            for p in range(2):
                gz_copy(d, s - 1, p).wait_recv()
                if s + 1 < lines:

                    @pl.when(inside(d))
                    def _():
                        gz_copy(d, s, p).start()

                gx_copy(j, p).start()
                c_near(j, p).start()

    def cross(j):
        @pl.when(valid(j))
        def _():
            for p in range(2):
                gx_copy(j, p).wait_recv()
                c_far(j, p).start()

    def project(j):
        d, s = slots[j]

        @pl.when(valid(j))
        def _():
            for p in range(2):
                c_near(j, p).wait_recv()
                c_far(j, p).wait_recv()
            first = pl.multiple_of(along(-d * s) * (4 * rows), 4 * rows)
            weight = w_ref[pl.ds(first, 4 * rows), :]
            kv_ref[pl.ds(first, 4 * rows), WINDOW:] = dot(
                weight, xt_ref[...], ((1,), (0,))
            ).astype(BF16)

            @pl.when(has_next)
            def _():
                kv_halo(along(-d * s)).start()

    def wait_kv_halo(line_):
        @pl.when(has_prev)
        def _():
            kv_halo(line_).wait_recv()

    key_idx = lax.broadcasted_iota(jnp.int32, (WINDOW, wide), 0)
    row_idx = lax.broadcasted_iota(jnp.int32, (WINDOW, wide), 1) % WINDOW
    older = key_idx > row_idx
    bias = jnp.where(has_prev, 0.0, NEG).astype(F32)
    groups = [1 - side, side, 3 - side, 2 + side]

    def key_rows(g, values):
        return pl.ds(pl.multiple_of(g * HEAD_DIM + values * KV_WIDTH, HEAD_DIM), HEAD_DIM)

    written = set()

    def band(k, t):
        g = groups[k]
        cols = pl.ds(pl.multiple_of(g * group_cols, group_cols), group_cols)
        here = slice(t * WINDOW, (t + 1) * WINDOW)
        span = slice(t * WINDOW, (t + 2) * WINDOW)
        q_t = q_ref[here, cols].T
        g_t = g_ref[here, cols].T
        pick = [slice(h * HEAD_DIM, (h + 1) * HEAD_DIM) for h in range(GROUP)]
        q_cat = jnp.concatenate([q_t[p] for p in pick], axis=1)
        g_cat = jnp.concatenate([g_t[p] for p in pick], axis=1)
        keys_t = kv_ref[key_rows(g, 0), span]
        values_t = kv_ref[key_rows(g, 1), span]
        s_all = dot(keys_t.T, q_cat, ((1,), (0,)))
        s_old = s_all[:WINDOW] + bias if t == 0 else s_all[:WINDOW]
        s = jnp.where(older, s_old, s_all[WINDOW:]) * (0.125 * LOG2E)
        p_all = dot(values_t.T, g_cat, ((1,), (0,)))
        grad_attn = jnp.where(older, p_all[:WINDOW], p_all[WINDOW:])
        sink = LOG2E * jnp.concatenate(
            [jnp.full((1, WINDOW), sink_ref[g * GROUP + h], F32) for h in range(GROUP)], axis=1
        )
        peak = jnp.maximum(jnp.max(s, axis=0, keepdims=True), sink)
        e = jnp.exp2(s - peak)
        norm = jnp.sum(e, axis=0, keepdims=True) + jnp.exp2(sink - peak)
        attn = e * (1.0 / norm)
        low = attn.astype(BF16)
        delta = jnp.sum(low.astype(F32) * grad_attn, axis=0, keepdims=True)
        d_s = (0.125 * attn * (grad_attn - delta)).astype(BF16)
        zero = jnp.zeros_like(low)
        low_all = jnp.concatenate([jnp.where(older, low, zero), jnp.where(older, zero, low)], axis=0)
        ds_all = jnp.concatenate([jnp.where(older, d_s, zero), jnp.where(older, zero, d_s)], axis=0)
        dq_cat = dot(keys_t, ds_all, ((1,), (0,))).astype(BF16)
        dq_t = jnp.concatenate(
            [dq_cat[:, h * WINDOW:(h + 1) * WINDOW] for h in range(GROUP)], axis=0
        )
        dq_ref[here, cols] = dq_t.T
        for values, (a, b) in enumerate(((q_cat, ds_all), (g_cat, low_all))):
            d_kv = dot(a, b, ((1,), (1,)))
            lo = slice(values * HEAD_DIM, (values + 1) * HEAD_DIM)
            for j in range(2):
                block = (k, lo, slice((t + j) * WINDOW, (t + j + 1) * WINDOW))
                grad = d_kv[:, j * WINDOW:(j + 1) * WINDOW]
                if (k, values, t + j) in written:
                    acc[block] += grad
                else:
                    acc[block] = grad
                    written.add((k, values, t + j))

    def halo(k):
        g = groups[k]
        return remote(h_out.at[g], h_in.at[g], hs.at[g], hr.at[g], before)

    def send_halo(k):
        @pl.when(has_prev)
        def _():
            h_out[groups[k]] = acc[k, :, :WINDOW].astype(BF16)
            halo(k).start()

    def c_copy(k):
        return remote(part.at[k, 1 - core], c_buf.at[k], cs.at[k], cr.at[k], c_peer)

    def finish(k):
        g = groups[k]
        last = slice(tok_count, tok_count + WINDOW)

        @pl.when(has_next)
        def _():
            halo(k).wait_recv()
            acc[k, :, last] += h_in[g].astype(F32)

        grads = acc[k, :, WINDOW:].astype(BF16)
        for values in range(2):
            gkv[key_rows(g, values), :] = grads[values * HEAD_DIM:(values + 1) * HEAD_DIM]
        chunk = dot(grads, x_ref[...], ((1,), (0,))).astype(BF16)
        for values in range(2):
            for core_ in range(2):
                lo = (2 * values + core_) * rows
                part[k, core_, values] = chunk[lo:lo + rows]
        c_copy(k).start()

    quarters = [(ch, p) for ch in range(2) for p in range(2)]

    def x_copy(a, ch, p):
        span = pl.ds(p * half, half)
        return remote(
            c_sum.at[2 * a, ch, span], x_buf.at[a, ch, span],
            xs.at[a, ch, p], xr.at[a, ch, p], x_peer,
        )

    def join(k):
        c_copy(k).wait_recv()
        for ch in (1, 0) if k == 2 else (0, 1):
            c_sum[k, ch] = (part[k, core, ch].astype(F32) + c_buf[k, ch].astype(F32)).astype(BF16)
            if k % 2 == 0:
                for p in range(2):
                    x_copy(k // 2, ch, p).start()

    def ends(a, ch):
        target = a + 2 * ch
        return target, {0: 3, 3: 0}.get(target), {0: 2, 3: 1}.get(target)

    def z_copy(a, ch, p):
        span = pl.ds(p * half, half)
        target, _, _ = ends(a, ch)
        return remote(
            z_out.at[a, ch, span], z_in.at[line, span],
            zs.at[a, ch, p], zr.at[line, p], at(target, side, core),
        )

    def t_copy(a, ch, p):
        span = pl.ds(p * half, half)
        _, _, middle = ends(a, ch)
        return remote(
            z_out.at[a, ch, span], t_in.at[span], zs.at[a, ch, p], tr.at[p], at(middle, side, core)
        )

    def joined(a, ch, p):
        span = slice(p * half, (p + 1) * half)
        return c_sum[2 * a + 1, ch, span].astype(F32) + x_buf[a, ch, span].astype(F32)

    def join_sides(a, ch, p):
        span = slice(p * half, (p + 1) * half)
        target, leaf, middle = ends(a, ch)
        x_copy(a, ch, p).wait_recv()

        @pl.when(line == target)
        def _():
            gw_ref[span, :] = joined(a, ch, p)

        plain = line != target
        if leaf is not None:
            plain = plain & (line != leaf) & (line != middle)

            @pl.when(line == leaf)
            def _():
                z_out[a, ch, span] = joined(a, ch, p).astype(BF16)
                t_copy(a, ch, p).start()

        @pl.when(plain)
        def _():
            z_out[a, ch, span] = joined(a, ch, p).astype(BF16)
            z_copy(a, ch, p).start()

    def join_lines(a, ch, p):
        span = slice(p * half, (p + 1) * half)
        _, leaf, middle = ends(a, ch)
        if leaf is None:
            return

        @pl.when(line == middle)
        def _():
            t_copy(a, ch, p).wait_recv()
            z_out[a, ch, span] = (joined(a, ch, p) + t_in[span].astype(F32)).astype(BF16)
            z_copy(a, ch, p).start()

    def input_rows(j):
        span = tok_count // 4
        sl = slice(j * span, (j + 1) * span)
        git_ref[:, sl] = dot(gkv[:, sl], w_ref[...], ((0,), (0,))).astype(BF16).T

    loads[0].wait()
    for p in range(2):
        for d in (1, -1):

            @pl.when(inside(d))
            def _():
                gz_copy(d, 0, p).start()

        gx_copy(0, p).start()
    for p in range(2):
        c_near(0, p).start()
    for p in range(2):
        piece(0, side, p)[...] = own_ref[p * half:(p + 1) * half, :]

    @pl.when(jnp.logical_not(has_prev))
    def _():
        kv_ref[:, :WINDOW] = jnp.zeros((kv_ref.shape[0], WINDOW), BF16)

    loads[1].wait()
    for k in range(tok_count // WINDOW):
        x_ref[k * WINDOW:(k + 1) * WINDOW, :] = xt_ref[:, k * WINDOW:(k + 1) * WINDOW].T
    steps = [[0]] + [[2 * s - 1, 2 * s] for s in range(1, lines)]
    for s in range(1, lines + 2):
        for stage, lag in ((land, 0), (cross, 1), (project, 2)):
            if 0 <= s - lag < lines:
                for j in steps[s - lag]:
                    stage(j)

    for load in loads[2:]:
        load.wait()
    band(0, 1)
    band(0, 2)
    wait_kv_halo(0)
    wait_kv_halo(2)
    band(1, 0)
    send_halo(1)
    band(0, 0)
    send_halo(0)
    for t in range(3, tiles):
        band(0, t)
    wait_kv_halo(1)
    wait_kv_halo(3)
    band(2, 0)
    send_halo(2)
    finish(0)
    band(3, 0)
    send_halo(3)
    join(0)
    for t in range(1, tiles):
        band(2, t)
    finish(2)
    band(1, 1)
    join(2)
    for t in range(2, tiles):
        band(1, t)
    finish(1)
    band(3, 1)
    join(1)
    for q in quarters:
        join_sides(0, *q)
    band(3, 2)
    join_lines(0, *quarters[0])
    band(3, 3)
    join_lines(0, *quarters[1])
    for t in range(4, tiles):
        band(3, t)
    finish(3)
    input_rows(0)
    join(3)
    later = [quarters[2], quarters[3], quarters[0], quarters[1]]
    for i, q in enumerate(later):
        join_sides(1, *q)
        if i < 3:
            input_rows(i + 1)
        if i:
            join_lines(1, *later[i - 1])
    join_lines(1, *later[3])

    for a in range(2):
        for ch in range(2):
            target, leaf, middle = ends(a, ch)

            @pl.when(line == target)
            def _():
                for source in range(lines):
                    if source not in (target, leaf):
                        for p in range(2):
                            span = slice(p * half, (p + 1) * half)
                            remote(
                                z_out.at[a, ch, pl.ds(p * half, half)],
                                z_in.at[source, pl.ds(p * half, half)],
                                zs.at[a, ch, p], zr.at[source, p], at(source, side, core),
                            ).wait_recv()
                            gw_ref[span, :] += z_in[source, span].astype(F32)

    for k in range(4):
        c_copy(k).wait_send()

        @pl.when(has_prev)
        def _():
            halo(k).wait_send()

    for a in range(2):
        for ch, p in quarters:
            x_copy(a, ch, p).wait_send()

            @pl.when(line != a + 2 * ch)
            def _():
                z_copy(a, ch, p).wait_send()

    for j, (d, s) in enumerate(slots):

        @pl.when(valid(j))
        def _():
            for p in range(2):
                if s + 1 < lines:
                    for d_ in (1, -1) if s == 0 else (d,):

                        @pl.when(inside(d_))
                        def _():
                            gz_copy(d_, s, p).wait_send()

                gx_copy(j, p).wait_send()
                c_near(j, p).wait_send()
                c_far(j, p).wait_send()

    for line_ in range(lines):

        @pl.when(has_next)
        def _():
            kv_halo(line_).wait_send()


def fused(sink_logits, queries, out_grad, inputs_t, kv_weight, count):
    lines = count // 4
    depth, tok_count = inputs_t.shape
    rows = kv_weight.shape[0]
    width = rows * count
    slots = len(line_slots(lines))
    dma = pltpu.SemaphoreType.DMA
    vmem = pl.BlockSpec(memory_space=pltpu.VMEM)
    hbm = pl.BlockSpec(memory_space=pltpu.HBM)

    def low(*shape):
        return pltpu.VMEM(shape, BF16)

    operands = [
        pltpu.with_memory_space_constraint(a, pltpu.HBM)
        for a in (sink_logits, queries, out_grad, inputs_t, kv_weight)
    ]
    return pl.pallas_call(
        fused_kernel,
        in_specs=[hbm] * 5,
        out_specs=(vmem, vmem, vmem),
        out_shape=(
            jax.ShapeDtypeStruct(queries.shape, BF16),
            jax.ShapeDtypeStruct((depth, tok_count), BF16),
            jax.ShapeDtypeStruct((rows, depth), F32),
        ),
        scratch_shapes=[
            pltpu.SMEM(sink_logits.shape, F32),
            low(*queries.shape),
            low(*queries.shape),
            low(depth, tok_count),
            low(tok_count, depth),
            low(rows, depth),
            low(width, depth),
            low(width, WINDOW + tok_count),
            pltpu.VMEM((KV_HEADS, 2 * HEAD_DIM, WINDOW + tok_count), F32),
            low(width, tok_count),
            low(KV_HEADS, 2 * HEAD_DIM, WINDOW),
            low(KV_HEADS, 2 * HEAD_DIM, WINDOW),
            low(4, 2, 2, rows, depth),
            low(4, 2, rows, depth),
            low(4, 2, rows, depth),
            low(2, 2, rows, depth),
            low(2, 2, rows, depth),
            low(lines, rows, depth),
            low(rows, depth),
            dma((5,)), dma((2, lines - 1, 2)), dma((2, lines - 1, 2)),
            dma((slots, 2)), dma((slots, 2)), dma((slots, 2, 2)), dma((slots, 2, 2)),
            dma((lines,)), dma((lines,)),
            dma((4,)), dma((4,)), dma((4,)), dma((4,)), dma((2, 2, 2)), dma((2, 2, 2)),
            dma((2, 2, 2)), dma((lines, 2)), dma((2,)),
        ],
        compiler_params=pltpu.CompilerParams(
            collective_id=0, has_side_effects=True, vmem_limit_bytes=48 << 20
        ),
        name="fused",
    )(*operands)


def store_kernel(dq_ref, git_ref, gw_ref, dq_hbm, git_hbm, gw_hbm, sems):
    copies = []
    for src, dst, cuts in ((git_ref, git_hbm, 3), (dq_ref, dq_hbm, 2), (gw_ref, gw_hbm, 1)):
        step = src.shape[0] // cuts
        for i in range(cuts):
            span = pl.ds(i * step, step)
            copies.append(pltpu.make_async_copy(src.at[span], dst.at[span], sems.at[len(copies)]))
    for copy in copies:
        copy.start()
    for copy in copies:
        copy.wait()


def store(*arrays):
    return pl.pallas_call(
        store_kernel,
        in_specs=[pl.BlockSpec(memory_space=pltpu.VMEM)] * 3,
        out_specs=[pl.BlockSpec(memory_space=pltpu.HBM)] * 3,
        out_shape=[jax.ShapeDtypeStruct(a.shape, a.dtype) for a in arrays],
        scratch_shapes=[pltpu.SemaphoreType.DMA((10,))],
        compiler_params=pltpu.CompilerParams(vmem_limit_bytes=8 << 20),
        name="store",
    )(*arrays)


def shards(inputs, queries, out_grad, kv_weight, sink_logits):
    index = lax.axis_index("ctx")
    count = lax.axis_size("ctx")
    rows = 2 * KV_WIDTH // count
    direct = count == 16 and kv_weight.shape[0] == rows and inputs.shape[0] % (4 * WINDOW) == 0
    if direct:
        inputs_t = inputs.T
        grad_queries, grad_input_t, grad_weight = fused(
            sink_logits, queries, out_grad, inputs_t, kv_weight, count
        )
        grad_queries, grad_input_t, grad_weight = store(grad_queries, grad_input_t, grad_weight)
        return (grad_queries, grad_input_t.T, grad_weight)
    full_weight = lax.all_gather(kv_weight, "ctx", axis=0, tiled=True)
    kv_rows = dot(inputs, full_weight, ((1,), (1,))).astype(BF16)
    kv_prev = shifted(kv_rows[-WINDOW:], "ctx", 1)
    kv_ext = jnp.concatenate([kv_prev, kv_rows], axis=0)
    sink_rows = jnp.repeat(sink_logits.reshape(KV_HEADS, GROUP), WINDOW, axis=1)
    grad_queries, grad_ext = band_grads(
        index.astype(jnp.int32).reshape(1), sink_rows, queries, out_grad, kv_ext
    )
    back = shifted(grad_ext[:WINDOW].astype(BF16), "ctx", -1).astype(F32)
    own = grad_ext[WINDOW:]
    grad_kv = jnp.concatenate([own[:-WINDOW], own[-WINDOW:] + back], axis=0).astype(BF16)
    partial = dot(grad_kv, inputs, ((0,), (0,))).astype(BF16)
    grad_weight = lax.psum_scatter(partial, "ctx", scatter_dimension=0, tiled=True).astype(F32)
    grad_input = dot(grad_kv, full_weight, ((1,), (0,))).astype(BF16)
    return (grad_queries, grad_input, grad_weight)


def solution(mesh):
    placed = P(("rep", "ctx"), None)
    return jax.shard_map(
        shards,
        mesh=mesh,
        in_specs=(placed, placed, placed, placed, P()),
        out_specs=(placed, placed, placed),
        check_vma=False,
    )
```

```python
import functools
import math

import jax
import jax.numpy as jnp
from jax import lax
from jax.experimental import pallas as pl
from jax.experimental.pallas import tpu as pltpu
from jax.sharding import PartitionSpec as P

HEADS = 32
KV_HEADS = 4
HEAD_DIM = 64
WINDOW = 128
GROUP = 8
KV_WIDTH = KV_HEADS * HEAD_DIM
LOG2E = math.log2(math.e)
NEG = -1e30
F32 = jnp.float32
BF16 = jnp.bfloat16


def shifted(block, axis, distance):
    devices = range(lax.axis_size(axis))
    route = [(i - distance, i) for i in devices if i - distance in devices]
    return lax.ppermute(block, axis, route)


def dot(a, b, contract):
    return lax.dot_general(a, b, (contract, ((), ())), preferred_element_type=F32)


def band_kernel(first_ref, sink_ref, q_ref, g_ref, kv_ref, dq_ref, dkv_ref):
    tile = pl.program_id(0)

    @pl.when(tile == 0)
    def _():
        dkv_ref[...] = jnp.zeros_like(dkv_ref)

    start = pl.multiple_of(tile * WINDOW, WINDOW)
    kv = kv_ref[pl.ds(start, 2 * WINDOW), :]
    wide = GROUP * WINDOW
    key_idx = lax.broadcasted_iota(jnp.int32, (WINDOW, wide), 0)
    row_idx = lax.broadcasted_iota(jnp.int32, (WINDOW, wide), 1) % WINDOW
    older = key_idx > row_idx
    bias = jnp.where((first_ref[0] == 0) & (tile == 0), NEG, 0.0).astype(F32)
    dk_parts, dv_parts = [], []
    for g in range(KV_HEADS):
        cols = slice(g * GROUP * HEAD_DIM, (g + 1) * GROUP * HEAD_DIM)
        q_t = q_ref[:, cols].T
        g_t = g_ref[:, cols].T
        pick = [slice(h * HEAD_DIM, (h + 1) * HEAD_DIM) for h in range(GROUP)]
        q_cat = jnp.concatenate([q_t[p] for p in pick], axis=1)
        g_cat = jnp.concatenate([g_t[p] for p in pick], axis=1)
        keys = kv[:, g * HEAD_DIM:(g + 1) * HEAD_DIM]
        values = kv[:, KV_WIDTH + g * HEAD_DIM:KV_WIDTH + (g + 1) * HEAD_DIM]
        s_all = dot(keys, q_cat, ((1,), (0,)))
        s = jnp.where(older, s_all[:WINDOW] + bias, s_all[WINDOW:]) * (0.125 * LOG2E)
        p_all = dot(values, g_cat, ((1,), (0,)))
        grad_attn = jnp.where(older, p_all[:WINDOW], p_all[WINDOW:])
        sink = sink_ref[g:g + 1, :] * LOG2E
        peak = jnp.maximum(jnp.max(s, axis=0, keepdims=True), sink)
        e = jnp.exp2(s - peak)
        norm = jnp.sum(e, axis=0, keepdims=True) + jnp.exp2(sink - peak)
        attn = e * (1.0 / norm)
        low = attn.astype(BF16)
        delta = jnp.sum(low.astype(F32) * grad_attn, axis=0, keepdims=True)
        d_s = (0.125 * attn * (grad_attn - delta)).astype(BF16)
        zero = jnp.zeros_like(low)
        low_all = jnp.concatenate([jnp.where(older, low, zero), jnp.where(older, zero, low)], axis=0)
        ds_all = jnp.concatenate([jnp.where(older, d_s, zero), jnp.where(older, zero, d_s)], axis=0)
        dq_cat = dot(keys.T, ds_all, ((1,), (0,))).astype(BF16)
        dq_t = jnp.concatenate(
            [dq_cat[:, h * WINDOW:(h + 1) * WINDOW] for h in range(GROUP)], axis=0
        )
        dq_ref[:, cols] = dq_t.T
        dk_parts.append(dot(ds_all, q_cat, ((1,), (1,))))
        dv_parts.append(dot(low_all, g_cat, ((1,), (1,))))
    dkv_ref[pl.ds(start, 2 * WINDOW), :] += jnp.concatenate(dk_parts + dv_parts, axis=1)


def band_grads(first, sink_rows, queries, out_grad, kv_ext):
    tok_count, width = queries.shape
    tiles = tok_count // WINDOW
    row_spec = pl.BlockSpec((WINDOW, width), lambda t: (t, 0))
    work = tok_count * 2 * WINDOW * HEADS * HEAD_DIM * 2 * 5
    return pl.pallas_call(
        band_kernel,
        grid=(tiles,),
        in_specs=[
            pl.BlockSpec(memory_space=pltpu.SMEM),
            pl.BlockSpec(sink_rows.shape, lambda t: (0, 0)),
            row_spec,
            row_spec,
            pl.BlockSpec(kv_ext.shape, lambda t: (0, 0)),
        ],
        out_specs=(row_spec, pl.BlockSpec(kv_ext.shape, lambda t: (0, 0))),
        out_shape=(
            jax.ShapeDtypeStruct(queries.shape, BF16),
            jax.ShapeDtypeStruct(kv_ext.shape, F32),
        ),
        compiler_params=pltpu.CompilerParams(
            dimension_semantics=("arbitrary",), vmem_limit_bytes=20 << 20
        ),
        cost_estimate=pl.CostEstimate(
            flops=work, bytes_accessed=6 * tok_count * width, transcendentals=0
        ),
        name="band_grads",
    )(
        first,
        sink_rows,
        queries,
        pltpu.with_memory_space_constraint(out_grad, pltpu.HBM),
        kv_ext,
    )


def peers(lines):
    me = lax.axis_index("ctx").astype(jnp.int32)
    line = lax.div(me, 4)
    side = lax.rem(lax.div(me, 2), 2)
    core = lax.rem(me, 2)

    def at(line_, side_, core_):
        return line_ * 4 + side_ * 2 + core_

    def along(step):
        return lax.rem(line + step + lines, lines)

    return line, side, core, at, along


def remote(src, dst, send_sem, recv_sem, target):
    return pltpu.make_async_remote_copy(
        src_ref=src,
        dst_ref=dst,
        send_sem=send_sem,
        recv_sem=recv_sem,
        device_id={"ctx": target},
        device_id_type=pl.DeviceIdType.MESH,
    )


def neighbours(lines):
    me = lax.axis_index("ctx").astype(jnp.int32)
    count = 4 * lines
    before, after = lax.rem(me + count - 1, count), lax.rem(me + 1, count)
    return me, me > 0, me < count - 1, before, after


def line_slots(lines):
    return [(0, 0)] + [(d, s) for s in range(1, lines) for d in (1, -1)]


def fused_kernel(
    sink_hbm, q_hbm, g_hbm, x_hbm, w_hbm, dq_ref, git_ref, gw_ref,
    sink_ref, q_ref, g_ref, xt_ref, x_ref, own_ref, w_ref, kv_ref,
    acc, gkv, h_out, h_in, part, c_buf, c_sum, x_buf, z_out, z_in, t_in,
    ls, gzs, gzr, gxs, gxr, gcs, gcr, ghs, ghr,
    hs, hr, cs, cr, xs, xr, zs, zr, tr,
):
    lines = 4
    loads = [
        pltpu.make_async_copy(src, dst, ls.at[i])
        for i, (src, dst) in enumerate(
            ((w_hbm, own_ref), (x_hbm, xt_ref), (q_hbm, q_ref), (g_hbm, g_ref), (sink_hbm, sink_ref))
        )
    ]
    for load in loads:
        load.start()
    rows = own_ref.shape[0]
    half = rows // 2
    tok_count = q_ref.shape[0]
    tiles = tok_count // WINDOW
    wide = GROUP * WINDOW
    group_cols = GROUP * HEAD_DIM
    line, side, core, at, along = peers(lines)
    x_peer = at(line, 1 - side, core)
    c_peer = at(line, side, 1 - core)
    _, has_prev, has_next, before, after = neighbours(lines)
    barrier = pltpu.get_barrier_semaphore()
    partners = [x_peer, c_peer] + [at(along(k), side, core) for k in range(1, lines)]
    for target in partners + [before, after]:
        pl.semaphore_signal(
            barrier, inc=1, device_id={"ctx": target}, device_id_type=pl.DeviceIdType.MESH
        )
    pl.semaphore_wait(barrier, len(partners) + 2)

    def inside(step):
        return (line + step >= 0) & (line + step < lines)

    def piece(step, side_, p):
        first = at(along(step), side_, core) * rows + p * half
        return w_ref.at[pl.ds(pl.multiple_of(first, half), half), :]

    def source(slot, p):
        d, s = slot
        return own_ref.at[pl.ds(p * half, half), :] if s == 0 else piece(-d * s, side, p)

    def gz_copy(d, s, p):
        i = (0 if d > 0 else 1, s, p)
        return remote(
            source((d, s), p), piece(-d * s, side, p), gzs.at[i], gzr.at[i],
            at(along(d), side, core),
        )

    slots = line_slots(lines)

    def gx_copy(j, p):
        d, s = slots[j]
        return remote(
            source(slots[j], p), piece(-d * s, side, p), gxs.at[j, p], gxr.at[j, p], x_peer
        )

    def c_near(j, p):
        d, s = slots[j]
        return remote(
            source(slots[j], p), piece(-d * s, side, p), gcs.at[j, 0, p], gcr.at[j, 0, p], c_peer
        )

    def c_far(j, p):
        d, s = slots[j]
        other = piece(-d * s, 1 - side, p)
        return remote(other, other, gcs.at[j, 1, p], gcr.at[j, 1, p], c_peer)

    def kv_halo(line_):
        chunk = pl.ds(pl.multiple_of(line_ * (4 * rows), 4 * rows), 4 * rows)
        return remote(
            kv_ref.at[chunk, pl.ds(tok_count, WINDOW)],
            kv_ref.at[chunk, pl.ds(0, WINDOW)],
            ghs.at[line_], ghr.at[line_], after,
        )

    def valid(j):
        d, s = slots[j]
        return inside(-d * s)

    def land(j):
        d, s = slots[j]

        @pl.when(valid(j))
        def _():
            for p in range(2):
                gz_copy(d, s - 1, p).wait_recv()
                if s + 1 < lines:

                    @pl.when(inside(d))
                    def _():
                        gz_copy(d, s, p).start()

                gx_copy(j, p).start()
                c_near(j, p).start()

    def cross(j):
        @pl.when(valid(j))
        def _():
            for p in range(2):
                gx_copy(j, p).wait_recv()
                c_far(j, p).start()

    def project(j):
        d, s = slots[j]

        @pl.when(valid(j))
        def _():
            for p in range(2):
                c_near(j, p).wait_recv()
                c_far(j, p).wait_recv()
            first = pl.multiple_of(along(-d * s) * (4 * rows), 4 * rows)
            weight = w_ref[pl.ds(first, 4 * rows), :]
            kv_ref[pl.ds(first, 4 * rows), WINDOW:] = dot(
                weight, xt_ref[...], ((1,), (0,))
            ).astype(BF16)

            @pl.when(has_next)
            def _():
                kv_halo(along(-d * s)).start()

    def wait_kv_halo(line_):
        @pl.when(has_prev)
        def _():
            kv_halo(line_).wait_recv()

    key_idx = lax.broadcasted_iota(jnp.int32, (WINDOW, wide), 0)
    row_idx = lax.broadcasted_iota(jnp.int32, (WINDOW, wide), 1) % WINDOW
    older = key_idx > row_idx
    bias = jnp.where(has_prev, 0.0, NEG).astype(F32)
    groups = [1 - side, side, 3 - side, 2 + side]

    def key_rows(g, values):
        return pl.ds(pl.multiple_of(g * HEAD_DIM + values * KV_WIDTH, HEAD_DIM), HEAD_DIM)

    written = set()

    def band(k, t):
        g = groups[k]
        cols = pl.ds(pl.multiple_of(g * group_cols, group_cols), group_cols)
        here = slice(t * WINDOW, (t + 1) * WINDOW)
        span = slice(t * WINDOW, (t + 2) * WINDOW)
        q_t = q_ref[here, cols].T
        g_t = g_ref[here, cols].T
        pick = [slice(h * HEAD_DIM, (h + 1) * HEAD_DIM) for h in range(GROUP)]
        q_cat = jnp.concatenate([q_t[p] for p in pick], axis=1)
        g_cat = jnp.concatenate([g_t[p] for p in pick], axis=1)
        keys_t = kv_ref[key_rows(g, 0), span]
        values_t = kv_ref[key_rows(g, 1), span]
        s_all = dot(keys_t.T, q_cat, ((1,), (0,)))
        s_old = s_all[:WINDOW] + bias if t == 0 else s_all[:WINDOW]
        s = jnp.where(older, s_old, s_all[WINDOW:]) * (0.125 * LOG2E)
        p_all = dot(values_t.T, g_cat, ((1,), (0,)))
        grad_attn = jnp.where(older, p_all[:WINDOW], p_all[WINDOW:])
        sink = LOG2E * jnp.concatenate(
            [jnp.full((1, WINDOW), sink_ref[g * GROUP + h], F32) for h in range(GROUP)], axis=1
        )
        peak = jnp.maximum(jnp.max(s, axis=0, keepdims=True), sink)
        e = jnp.exp2(s - peak)
        norm = jnp.sum(e, axis=0, keepdims=True) + jnp.exp2(sink - peak)
        attn = e * (1.0 / norm)
        low = attn.astype(BF16)
        delta = jnp.sum(low.astype(F32) * grad_attn, axis=0, keepdims=True)
        d_s = (0.125 * attn * (grad_attn - delta)).astype(BF16)
        zero = jnp.zeros_like(low)
        low_all = jnp.concatenate([jnp.where(older, low, zero), jnp.where(older, zero, low)], axis=0)
        ds_all = jnp.concatenate([jnp.where(older, d_s, zero), jnp.where(older, zero, d_s)], axis=0)
        dq_cat = dot(keys_t, ds_all, ((1,), (0,))).astype(BF16)
        dq_t = jnp.concatenate(
            [dq_cat[:, h * WINDOW:(h + 1) * WINDOW] for h in range(GROUP)], axis=0
        )
        dq_ref[here, cols] = dq_t.T
        for values, (a, b) in enumerate(((q_cat, ds_all), (g_cat, low_all))):
            d_kv = dot(a, b, ((1,), (1,)))
            lo = slice(values * HEAD_DIM, (values + 1) * HEAD_DIM)
            for j in range(2):
                block = (k, lo, slice((t + j) * WINDOW, (t + j + 1) * WINDOW))
                grad = d_kv[:, j * WINDOW:(j + 1) * WINDOW]
                if (k, values, t + j) in written:
                    acc[block] += grad
                else:
                    acc[block] = grad
                    written.add((k, values, t + j))

    def halo(k):
        g = groups[k]
        return remote(h_out.at[g], h_in.at[g], hs.at[g], hr.at[g], before)

    def send_halo(k):
        @pl.when(has_prev)
        def _():
            h_out[groups[k]] = acc[k, :, :WINDOW].astype(BF16)
            halo(k).start()

    def c_copy(k):
        return remote(part.at[k, 1 - core], c_buf.at[k], cs.at[k], cr.at[k], c_peer)

    def finish(k):
        g = groups[k]
        last = slice(tok_count, tok_count + WINDOW)

        @pl.when(has_next)
        def _():
            halo(k).wait_recv()
            acc[k, :, last] += h_in[g].astype(F32)

        grads = acc[k, :, WINDOW:].astype(BF16)
        for values in range(2):
            gkv[key_rows(g, values), :] = grads[values * HEAD_DIM:(values + 1) * HEAD_DIM]
        chunk = dot(grads, x_ref[...], ((1,), (0,))).astype(BF16)
        for values in range(2):
            for core_ in range(2):
                lo = (2 * values + core_) * rows
                part[k, core_, values] = chunk[lo:lo + rows]
        c_copy(k).start()

    quarters = [(ch, p) for ch in range(2) for p in range(2)]
    later = [quarters[2], quarters[0], quarters[3], quarters[1]]

    def x_copy(a, ch, p):
        span = pl.ds(p * half, half)
        return remote(
            c_sum.at[2 * a, ch, span], x_buf.at[a, ch, span],
            xs.at[a, ch, p], xr.at[a, ch, p], x_peer,
        )

    def join(k):
        c_copy(k).wait_recv()
        for ch in range(2):
            c_sum[k, ch] = (part[k, core, ch].astype(F32) + c_buf[k, ch].astype(F32)).astype(BF16)
        if k % 2 == 0:
            for ch, p in quarters if k == 0 else later:
                x_copy(k // 2, ch, p).start()

    def ends(a, ch):
        target = a + 2 * ch
        return target, {0: 3, 3: 0}.get(target), {0: 2, 3: 1}.get(target)

    def z_copy(a, ch, p):
        span = pl.ds(p * half, half)
        target, _, _ = ends(a, ch)
        return remote(
            z_out.at[a, ch, span], z_in.at[line, span],
            zs.at[a, ch, p], zr.at[line, p], at(target, side, core),
        )

    def t_copy(a, ch, p):
        span = pl.ds(p * half, half)
        _, _, middle = ends(a, ch)
        return remote(
            z_out.at[a, ch, span], t_in.at[span], zs.at[a, ch, p], tr.at[p], at(middle, side, core)
        )

    def joined(a, ch, p):
        span = slice(p * half, (p + 1) * half)
        return c_sum[2 * a + 1, ch, span].astype(F32) + x_buf[a, ch, span].astype(F32)

    def join_sides(a, ch, p):
        span = slice(p * half, (p + 1) * half)
        target, leaf, middle = ends(a, ch)
        x_copy(a, ch, p).wait_recv()

        @pl.when(line == target)
        def _():
            gw_ref[span, :] = joined(a, ch, p)

        plain = line != target
        if leaf is not None:
            plain = plain & (line != leaf) & (line != middle)

            @pl.when(line == leaf)
            def _():
                z_out[a, ch, span] = joined(a, ch, p).astype(BF16)
                t_copy(a, ch, p).start()

        @pl.when(plain)
        def _():
            z_out[a, ch, span] = joined(a, ch, p).astype(BF16)
            z_copy(a, ch, p).start()

    def join_lines(a, ch, p):
        span = slice(p * half, (p + 1) * half)
        _, leaf, middle = ends(a, ch)
        if leaf is None:
            return

        @pl.when(line == middle)
        def _():
            t_copy(a, ch, p).wait_recv()
            z_out[a, ch, span] = (joined(a, ch, p) + t_in[span].astype(F32)).astype(BF16)
            z_copy(a, ch, p).start()

    def input_rows(j):
        span = tok_count // 4
        sl = slice(j * span, (j + 1) * span)
        git_ref[:, sl] = dot(gkv[:, sl], w_ref[...], ((0,), (0,))).astype(BF16).T

    loads[0].wait()
    for p in range(2):
        for d in (1, -1):

            @pl.when(inside(d))
            def _():
                gz_copy(d, 0, p).start()

        gx_copy(0, p).start()
    for p in range(2):
        c_near(0, p).start()
    for p in range(2):
        piece(0, side, p)[...] = own_ref[p * half:(p + 1) * half, :]

    @pl.when(jnp.logical_not(has_prev))
    def _():
        kv_ref[:, :WINDOW] = jnp.zeros((kv_ref.shape[0], WINDOW), BF16)

    loads[1].wait()
    for k in range(tok_count // WINDOW):
        x_ref[k * WINDOW:(k + 1) * WINDOW, :] = xt_ref[:, k * WINDOW:(k + 1) * WINDOW].T
    steps = [[0]] + [[2 * s - 1, 2 * s] for s in range(1, lines)]
    for s in range(1, lines + 2):
        for stage, lag in ((land, 0), (cross, 1), (project, 2)):
            if 0 <= s - lag < lines:
                for j in steps[s - lag]:
                    stage(j)

    for load in loads[2:]:
        load.wait()
    band(0, 1)
    band(0, 2)
    wait_kv_halo(0)
    wait_kv_halo(2)
    band(1, 0)
    send_halo(1)
    band(0, 0)
    send_halo(0)
    for t in range(3, tiles):
        band(0, t)
    wait_kv_halo(1)
    wait_kv_halo(3)
    band(2, 0)
    send_halo(2)
    finish(0)
    band(3, 0)
    send_halo(3)
    join(0)
    for t in range(1, tiles):
        band(1, t)
    finish(1)
    band(2, 1)
    join(1)
    join_sides(0, *quarters[0])
    band(2, 2)
    join_sides(0, *quarters[1])
    for t in range(3, tiles):
        band(2, t)
    finish(2)
    join_sides(0, *quarters[2])
    join_lines(0, *quarters[0])
    band(3, 1)
    join(2)
    join_sides(0, *quarters[3])
    join_lines(0, *quarters[1])
    band(3, 2)
    band(3, 3)
    for t in range(4, tiles):
        band(3, t)
    finish(3)
    input_rows(0)
    join(3)
    for i, q in enumerate(later):
        join_sides(1, *q)
        if i < 3:
            input_rows(i + 1)
        if i:
            join_lines(1, *later[i - 1])
    join_lines(1, *later[3])

    for a in range(2):
        for ch in range(2):
            target, leaf, middle = ends(a, ch)

            @pl.when(line == target)
            def _():
                for source in range(lines):
                    if source not in (target, leaf):
                        for p in range(2):
                            span = slice(p * half, (p + 1) * half)
                            remote(
                                z_out.at[a, ch, pl.ds(p * half, half)],
                                z_in.at[source, pl.ds(p * half, half)],
                                zs.at[a, ch, p], zr.at[source, p], at(source, side, core),
                            ).wait_recv()
                            gw_ref[span, :] += z_in[source, span].astype(F32)

    for k in range(4):
        c_copy(k).wait_send()

        @pl.when(has_prev)
        def _():
            halo(k).wait_send()

    for a in range(2):
        for ch, p in quarters:
            x_copy(a, ch, p).wait_send()

            @pl.when(line != a + 2 * ch)
            def _():
                z_copy(a, ch, p).wait_send()

    for j, (d, s) in enumerate(slots):

        @pl.when(valid(j))
        def _():
            for p in range(2):
                if s + 1 < lines:
                    for d_ in (1, -1) if s == 0 else (d,):

                        @pl.when(inside(d_))
                        def _():
                            gz_copy(d_, s, p).wait_send()

                gx_copy(j, p).wait_send()
                c_near(j, p).wait_send()
                c_far(j, p).wait_send()

    for line_ in range(lines):

        @pl.when(has_next)
        def _():
            kv_halo(line_).wait_send()


def fused(sink_logits, queries, out_grad, inputs_t, kv_weight, count):
    lines = count // 4
    depth, tok_count = inputs_t.shape
    rows = kv_weight.shape[0]
    width = rows * count
    slots = len(line_slots(lines))
    dma = pltpu.SemaphoreType.DMA
    vmem = pl.BlockSpec(memory_space=pltpu.VMEM)
    hbm = pl.BlockSpec(memory_space=pltpu.HBM)

    def low(*shape):
        return pltpu.VMEM(shape, BF16)

    operands = [
        pltpu.with_memory_space_constraint(a, pltpu.HBM)
        for a in (sink_logits, queries, out_grad, inputs_t, kv_weight)
    ]
    return pl.pallas_call(
        fused_kernel,
        in_specs=[hbm] * 5,
        out_specs=(vmem, vmem, vmem),
        out_shape=(
            jax.ShapeDtypeStruct(queries.shape, BF16),
            jax.ShapeDtypeStruct((depth, tok_count), BF16),
            jax.ShapeDtypeStruct((rows, depth), F32),
        ),
        scratch_shapes=[
            pltpu.SMEM(sink_logits.shape, F32),
            low(*queries.shape),
            low(*queries.shape),
            low(depth, tok_count),
            low(tok_count, depth),
            low(rows, depth),
            low(width, depth),
            low(width, WINDOW + tok_count),
            pltpu.VMEM((KV_HEADS, 2 * HEAD_DIM, WINDOW + tok_count), F32),
            low(width, tok_count),
            low(KV_HEADS, 2 * HEAD_DIM, WINDOW),
            low(KV_HEADS, 2 * HEAD_DIM, WINDOW),
            low(4, 2, 2, rows, depth),
            low(4, 2, rows, depth),
            low(4, 2, rows, depth),
            low(2, 2, rows, depth),
            low(2, 2, rows, depth),
            low(lines, rows, depth),
            low(rows, depth),
            dma((5,)), dma((2, lines - 1, 2)), dma((2, lines - 1, 2)),
            dma((slots, 2)), dma((slots, 2)), dma((slots, 2, 2)), dma((slots, 2, 2)),
            dma((lines,)), dma((lines,)),
            dma((4,)), dma((4,)), dma((4,)), dma((4,)), dma((2, 2, 2)), dma((2, 2, 2)),
            dma((2, 2, 2)), dma((lines, 2)), dma((2,)),
        ],
        compiler_params=pltpu.CompilerParams(
            collective_id=0, has_side_effects=True, vmem_limit_bytes=48 << 20
        ),
        name="fused",
    )(*operands)


def store_kernel(dq_ref, git_ref, gw_ref, dq_hbm, git_hbm, gw_hbm, sems):
    copies = []
    for src, dst, cuts in ((git_ref, git_hbm, 3), (dq_ref, dq_hbm, 2), (gw_ref, gw_hbm, 1)):
        step = src.shape[0] // cuts
        for i in range(cuts):
            span = pl.ds(i * step, step)
            copies.append(pltpu.make_async_copy(src.at[span], dst.at[span], sems.at[len(copies)]))
    for copy in copies:
        copy.start()
    for copy in copies:
        copy.wait()


def store(*arrays):
    return pl.pallas_call(
        store_kernel,
        in_specs=[pl.BlockSpec(memory_space=pltpu.VMEM)] * 3,
        out_specs=[pl.BlockSpec(memory_space=pltpu.HBM)] * 3,
        out_shape=[jax.ShapeDtypeStruct(a.shape, a.dtype) for a in arrays],
        scratch_shapes=[pltpu.SemaphoreType.DMA((10,))],
        compiler_params=pltpu.CompilerParams(vmem_limit_bytes=8 << 20),
        name="store",
    )(*arrays)


def shards(inputs, queries, out_grad, kv_weight, sink_logits):
    index = lax.axis_index("ctx")
    count = lax.axis_size("ctx")
    rows = 2 * KV_WIDTH // count
    direct = count == 16 and kv_weight.shape[0] == rows and inputs.shape[0] % (4 * WINDOW) == 0
    if direct:
        inputs_t = inputs.T
        grad_queries, grad_input_t, grad_weight = fused(
            sink_logits, queries, out_grad, inputs_t, kv_weight, count
        )
        grad_queries, grad_input_t, grad_weight = store(grad_queries, grad_input_t, grad_weight)
        return (grad_queries, grad_input_t.T, grad_weight)
    full_weight = lax.all_gather(kv_weight, "ctx", axis=0, tiled=True)
    kv_rows = dot(inputs, full_weight, ((1,), (1,))).astype(BF16)
    kv_prev = shifted(kv_rows[-WINDOW:], "ctx", 1)
    kv_ext = jnp.concatenate([kv_prev, kv_rows], axis=0)
    sink_rows = jnp.repeat(sink_logits.reshape(KV_HEADS, GROUP), WINDOW, axis=1)
    grad_queries, grad_ext = band_grads(
        index.astype(jnp.int32).reshape(1), sink_rows, queries, out_grad, kv_ext
    )
    back = shifted(grad_ext[:WINDOW].astype(BF16), "ctx", -1).astype(F32)
    own = grad_ext[WINDOW:]
    grad_kv = jnp.concatenate([own[:-WINDOW], own[-WINDOW:] + back], axis=0).astype(BF16)
    partial = dot(grad_kv, inputs, ((0,), (0,))).astype(BF16)
    grad_weight = lax.psum_scatter(partial, "ctx", scatter_dimension=0, tiled=True).astype(F32)
    grad_input = dot(grad_kv, full_weight, ((1,), (0,))).astype(BF16)
    return (grad_queries, grad_input, grad_weight)


def solution(mesh):
    placed = P(("rep", "ctx"), None)
    return jax.shard_map(
        shards,
        mesh=mesh,
        in_specs=(placed, placed, placed, placed, P()),
        out_specs=(placed, placed, placed),
        check_vma=False,
    )
```

```python
import functools
import math

import jax
import jax.numpy as jnp
from jax import lax
from jax.experimental import pallas as pl
from jax.experimental.pallas import tpu as pltpu
from jax.sharding import PartitionSpec as P

HEADS = 32
KV_HEADS = 4
HEAD_DIM = 64
WINDOW = 128
GROUP = 8
KV_WIDTH = KV_HEADS * HEAD_DIM
LOG2E = math.log2(math.e)
NEG = -1e30
F32 = jnp.float32
BF16 = jnp.bfloat16


def shifted(block, axis, distance):
    devices = range(lax.axis_size(axis))
    route = [(i - distance, i) for i in devices if i - distance in devices]
    return lax.ppermute(block, axis, route)


def dot(a, b, contract):
    return lax.dot_general(a, b, (contract, ((), ())), preferred_element_type=F32)


def band_kernel(first_ref, sink_ref, q_ref, g_ref, kv_ref, dq_ref, dkv_ref):
    tile = pl.program_id(0)

    @pl.when(tile == 0)
    def _():
        dkv_ref[...] = jnp.zeros_like(dkv_ref)

    start = pl.multiple_of(tile * WINDOW, WINDOW)
    kv = kv_ref[pl.ds(start, 2 * WINDOW), :]
    wide = GROUP * WINDOW
    key_idx = lax.broadcasted_iota(jnp.int32, (WINDOW, wide), 0)
    row_idx = lax.broadcasted_iota(jnp.int32, (WINDOW, wide), 1) % WINDOW
    older = key_idx > row_idx
    bias = jnp.where((first_ref[0] == 0) & (tile == 0), NEG, 0.0).astype(F32)
    dk_parts, dv_parts = [], []
    for g in range(KV_HEADS):
        cols = slice(g * GROUP * HEAD_DIM, (g + 1) * GROUP * HEAD_DIM)
        q_t = q_ref[:, cols].T
        g_t = g_ref[:, cols].T
        pick = [slice(h * HEAD_DIM, (h + 1) * HEAD_DIM) for h in range(GROUP)]
        q_cat = jnp.concatenate([q_t[p] for p in pick], axis=1)
        g_cat = jnp.concatenate([g_t[p] for p in pick], axis=1)
        keys = kv[:, g * HEAD_DIM:(g + 1) * HEAD_DIM]
        values = kv[:, KV_WIDTH + g * HEAD_DIM:KV_WIDTH + (g + 1) * HEAD_DIM]
        s_all = dot(keys, q_cat, ((1,), (0,)))
        s = jnp.where(older, s_all[:WINDOW] + bias, s_all[WINDOW:]) * (0.125 * LOG2E)
        p_all = dot(values, g_cat, ((1,), (0,)))
        grad_attn = jnp.where(older, p_all[:WINDOW], p_all[WINDOW:])
        sink = sink_ref[g:g + 1, :] * LOG2E
        peak = jnp.maximum(jnp.max(s, axis=0, keepdims=True), sink)
        e = jnp.exp2(s - peak)
        norm = jnp.sum(e, axis=0, keepdims=True) + jnp.exp2(sink - peak)
        attn = e * (1.0 / norm)
        low = attn.astype(BF16)
        delta = jnp.sum(low.astype(F32) * grad_attn, axis=0, keepdims=True)
        d_s = (0.125 * attn * (grad_attn - delta)).astype(BF16)
        zero = jnp.zeros_like(low)
        low_all = jnp.concatenate([jnp.where(older, low, zero), jnp.where(older, zero, low)], axis=0)
        ds_all = jnp.concatenate([jnp.where(older, d_s, zero), jnp.where(older, zero, d_s)], axis=0)
        dq_cat = dot(keys.T, ds_all, ((1,), (0,))).astype(BF16)
        dq_t = jnp.concatenate(
            [dq_cat[:, h * WINDOW:(h + 1) * WINDOW] for h in range(GROUP)], axis=0
        )
        dq_ref[:, cols] = dq_t.T
        dk_parts.append(dot(ds_all, q_cat, ((1,), (1,))))
        dv_parts.append(dot(low_all, g_cat, ((1,), (1,))))
    dkv_ref[pl.ds(start, 2 * WINDOW), :] += jnp.concatenate(dk_parts + dv_parts, axis=1)


def band_grads(first, sink_rows, queries, out_grad, kv_ext):
    tok_count, width = queries.shape
    tiles = tok_count // WINDOW
    row_spec = pl.BlockSpec((WINDOW, width), lambda t: (t, 0))
    work = tok_count * 2 * WINDOW * HEADS * HEAD_DIM * 2 * 5
    return pl.pallas_call(
        band_kernel,
        grid=(tiles,),
        in_specs=[
            pl.BlockSpec(memory_space=pltpu.SMEM),
            pl.BlockSpec(sink_rows.shape, lambda t: (0, 0)),
            row_spec,
            row_spec,
            pl.BlockSpec(kv_ext.shape, lambda t: (0, 0)),
        ],
        out_specs=(row_spec, pl.BlockSpec(kv_ext.shape, lambda t: (0, 0))),
        out_shape=(
            jax.ShapeDtypeStruct(queries.shape, BF16),
            jax.ShapeDtypeStruct(kv_ext.shape, F32),
        ),
        compiler_params=pltpu.CompilerParams(
            dimension_semantics=("arbitrary",), vmem_limit_bytes=20 << 20
        ),
        cost_estimate=pl.CostEstimate(
            flops=work, bytes_accessed=6 * tok_count * width, transcendentals=0
        ),
        name="band_grads",
    )(
        first,
        sink_rows,
        queries,
        pltpu.with_memory_space_constraint(out_grad, pltpu.HBM),
        kv_ext,
    )


def peers(lines):
    me = lax.axis_index("ctx").astype(jnp.int32)
    line = lax.div(me, 4)
    side = lax.rem(lax.div(me, 2), 2)
    core = lax.rem(me, 2)

    def at(line_, side_, core_):
        return line_ * 4 + side_ * 2 + core_

    def along(step):
        return lax.rem(line + step + lines, lines)

    return line, side, core, at, along


def remote(src, dst, send_sem, recv_sem, target):
    return pltpu.make_async_remote_copy(
        src_ref=src,
        dst_ref=dst,
        send_sem=send_sem,
        recv_sem=recv_sem,
        device_id={"ctx": target},
        device_id_type=pl.DeviceIdType.MESH,
    )


def neighbours(lines):
    me = lax.axis_index("ctx").astype(jnp.int32)
    count = 4 * lines
    before, after = lax.rem(me + count - 1, count), lax.rem(me + 1, count)
    return me, me > 0, me < count - 1, before, after


def line_slots(lines):
    return [(0, 0)] + [(d, s) for s in range(1, lines) for d in (1, -1)]


def fused_kernel(
    sink_hbm, q_hbm, g_hbm, x_hbm, w_hbm, dq_ref, git_ref, gw_ref,
    sink_ref, q_ref, g_ref, xt_ref, x_ref, own_ref, w_ref, kv_ref,
    acc, gkv, h_out, h_in, part, c_buf, c_sum, x_buf, z_out, z_in, t_in,
    ls, gzs, gzr, gxs, gxr, gcs, gcr, ghs, ghr,
    hs, hr, cs, cr, xs, xr, zs, zr, tr,
):
    lines = 4
    loads = [
        pltpu.make_async_copy(src, dst, ls.at[i])
        for i, (src, dst) in enumerate(
            ((w_hbm, own_ref), (x_hbm, xt_ref), (q_hbm, q_ref), (g_hbm, g_ref), (sink_hbm, sink_ref))
        )
    ]
    for load in loads:
        load.start()
    rows = own_ref.shape[0]
    half = rows // 2
    tok_count = q_ref.shape[0]
    tiles = tok_count // WINDOW
    wide = GROUP * WINDOW
    group_cols = GROUP * HEAD_DIM
    line, side, core, at, along = peers(lines)
    x_peer = at(line, 1 - side, core)
    c_peer = at(line, side, 1 - core)
    _, has_prev, has_next, before, after = neighbours(lines)
    barrier = pltpu.get_barrier_semaphore()
    partners = [x_peer, c_peer] + [at(along(k), side, core) for k in range(1, lines)]
    for target in partners + [before, after]:
        pl.semaphore_signal(
            barrier, inc=1, device_id={"ctx": target}, device_id_type=pl.DeviceIdType.MESH
        )
    pl.semaphore_wait(barrier, len(partners) + 2)

    def inside(step):
        return (line + step >= 0) & (line + step < lines)

    def piece(step, side_, p):
        first = at(along(step), side_, core) * rows + p * half
        return w_ref.at[pl.ds(pl.multiple_of(first, half), half), :]

    def source(slot, p):
        d, s = slot
        return own_ref.at[pl.ds(p * half, half), :] if s == 0 else piece(-d * s, side, p)

    def gz_copy(d, s, p):
        i = (0 if d > 0 else 1, s, p)
        return remote(
            source((d, s), p), piece(-d * s, side, p), gzs.at[i], gzr.at[i],
            at(along(d), side, core),
        )

    slots = line_slots(lines)

    def gx_copy(j, p):
        d, s = slots[j]
        return remote(
            source(slots[j], p), piece(-d * s, side, p), gxs.at[j, p], gxr.at[j, p], x_peer
        )

    def c_near(j, p):
        d, s = slots[j]
        return remote(
            source(slots[j], p), piece(-d * s, side, p), gcs.at[j, 0, p], gcr.at[j, 0, p], c_peer
        )

    def c_far(j, p):
        d, s = slots[j]
        other = piece(-d * s, 1 - side, p)
        return remote(other, other, gcs.at[j, 1, p], gcr.at[j, 1, p], c_peer)

    def kv_halo(line_):
        chunk = pl.ds(pl.multiple_of(line_ * (4 * rows), 4 * rows), 4 * rows)
        return remote(
            kv_ref.at[chunk, pl.ds(tok_count, WINDOW)],
            kv_ref.at[chunk, pl.ds(0, WINDOW)],
            ghs.at[line_], ghr.at[line_], after,
        )

    def valid(j):
        d, s = slots[j]
        return inside(-d * s)

    def land(j):
        d, s = slots[j]

        @pl.when(valid(j))
        def _():
            for p in range(2):
                gz_copy(d, s - 1, p).wait_recv()
                if s + 1 < lines:

                    @pl.when(inside(d))
                    def _():
                        gz_copy(d, s, p).start()

                gx_copy(j, p).start()
                c_near(j, p).start()

    def cross(j):
        @pl.when(valid(j))
        def _():
            for p in range(2):
                gx_copy(j, p).wait_recv()
                c_far(j, p).start()

    def project(j):
        d, s = slots[j]

        @pl.when(valid(j))
        def _():
            for p in range(2):
                c_near(j, p).wait_recv()
                c_far(j, p).wait_recv()
            first = pl.multiple_of(along(-d * s) * (4 * rows), 4 * rows)
            weight = w_ref[pl.ds(first, 4 * rows), :]
            kv_ref[pl.ds(first, 4 * rows), WINDOW:] = dot(
                weight, xt_ref[...], ((1,), (0,))
            ).astype(BF16)

            @pl.when(has_next)
            def _():
                kv_halo(along(-d * s)).start()

    def wait_kv_halo(line_):
        @pl.when(has_prev)
        def _():
            kv_halo(line_).wait_recv()

    key_idx = lax.broadcasted_iota(jnp.int32, (WINDOW, wide), 0)
    row_idx = lax.broadcasted_iota(jnp.int32, (WINDOW, wide), 1) % WINDOW
    older = key_idx > row_idx
    bias = jnp.where(has_prev, 0.0, NEG).astype(F32)
    groups = [1 - side, side, 3 - side, 2 + side]

    def key_rows(g, values):
        return pl.ds(pl.multiple_of(g * HEAD_DIM + values * KV_WIDTH, HEAD_DIM), HEAD_DIM)

    written = set()

    def band(k, t):
        g = groups[k]
        cols = pl.ds(pl.multiple_of(g * group_cols, group_cols), group_cols)
        here = slice(t * WINDOW, (t + 1) * WINDOW)
        span = slice(t * WINDOW, (t + 2) * WINDOW)
        q_t = q_ref[here, cols].T
        g_t = g_ref[here, cols].T
        pick = [slice(h * HEAD_DIM, (h + 1) * HEAD_DIM) for h in range(GROUP)]
        q_cat = jnp.concatenate([q_t[p] for p in pick], axis=1)
        g_cat = jnp.concatenate([g_t[p] for p in pick], axis=1)
        keys_t = kv_ref[key_rows(g, 0), span]
        values_t = kv_ref[key_rows(g, 1), span]
        s_all = dot(keys_t.T, q_cat, ((1,), (0,)))
        s_old = s_all[:WINDOW] + bias if t == 0 else s_all[:WINDOW]
        s = jnp.where(older, s_old, s_all[WINDOW:]) * (0.125 * LOG2E)
        p_all = dot(values_t.T, g_cat, ((1,), (0,)))
        grad_attn = jnp.where(older, p_all[:WINDOW], p_all[WINDOW:])
        sink = LOG2E * jnp.concatenate(
            [jnp.full((1, WINDOW), sink_ref[g * GROUP + h], F32) for h in range(GROUP)], axis=1
        )
        peak = jnp.maximum(jnp.max(s, axis=0, keepdims=True), sink)
        e = jnp.exp2(s - peak)
        norm = jnp.sum(e, axis=0, keepdims=True) + jnp.exp2(sink - peak)
        attn = e * (1.0 / norm)
        low = attn.astype(BF16)
        delta = jnp.sum(low.astype(F32) * grad_attn, axis=0, keepdims=True)
        d_s = (0.125 * attn * (grad_attn - delta)).astype(BF16)
        zero = jnp.zeros_like(low)
        low_all = jnp.concatenate([jnp.where(older, low, zero), jnp.where(older, zero, low)], axis=0)
        ds_all = jnp.concatenate([jnp.where(older, d_s, zero), jnp.where(older, zero, d_s)], axis=0)
        dq_cat = dot(keys_t, ds_all, ((1,), (0,))).astype(BF16)
        dq_t = jnp.concatenate(
            [dq_cat[:, h * WINDOW:(h + 1) * WINDOW] for h in range(GROUP)], axis=0
        )
        dq_ref[here, cols] = dq_t.T
        for values, (a, b) in enumerate(((q_cat, ds_all), (g_cat, low_all))):
            d_kv = dot(a, b, ((1,), (1,)))
            lo = slice(values * HEAD_DIM, (values + 1) * HEAD_DIM)
            for j in range(2):
                block = (k, lo, slice((t + j) * WINDOW, (t + j + 1) * WINDOW))
                grad = d_kv[:, j * WINDOW:(j + 1) * WINDOW]
                if (k, values, t + j) in written:
                    acc[block] += grad
                else:
                    acc[block] = grad
                    written.add((k, values, t + j))

    def halo(k):
        g = groups[k]
        return remote(h_out.at[g], h_in.at[g], hs.at[g], hr.at[g], before)

    def send_halo(k):
        @pl.when(has_prev)
        def _():
            h_out[groups[k]] = acc[k, :, :WINDOW].astype(BF16)
            halo(k).start()

    def c_copy(k):
        return remote(part.at[k, 1 - core], c_buf.at[k], cs.at[k], cr.at[k], c_peer)

    def finish(k):
        g = groups[k]
        last = slice(tok_count, tok_count + WINDOW)

        @pl.when(has_next)
        def _():
            halo(k).wait_recv()
            acc[k, :, last] += h_in[g].astype(F32)

        grads = acc[k, :, WINDOW:].astype(BF16)
        for values in range(2):
            gkv[key_rows(g, values), :] = grads[values * HEAD_DIM:(values + 1) * HEAD_DIM]
        chunk = dot(grads, x_ref[...], ((1,), (0,))).astype(BF16)
        for values in range(2):
            for core_ in range(2):
                lo = (2 * values + core_) * rows
                part[k, core_, values] = chunk[lo:lo + rows]
        c_copy(k).start()

    quarters = [(ch, p) for ch in range(2) for p in range(2)]
    early = [quarters[0], quarters[2], quarters[1], quarters[3]]
    later = [quarters[2], quarters[0], quarters[3], quarters[1]]

    def x_copy(a, ch, p):
        span = pl.ds(p * half, half)
        return remote(
            c_sum.at[2 * a, ch, span], x_buf.at[a, ch, span],
            xs.at[a, ch, p], xr.at[a, ch, p], x_peer,
        )

    def join(k):
        c_copy(k).wait_recv()
        for ch in range(2):
            c_sum[k, ch] = (part[k, core, ch].astype(F32) + c_buf[k, ch].astype(F32)).astype(BF16)
        if k % 2 == 0:
            for ch, p in early if k == 0 else later:
                x_copy(k // 2, ch, p).start()

    def ends(a, ch):
        target = a + 2 * ch
        return target, {0: 3, 3: 0}.get(target), {0: 2, 3: 1}.get(target)

    def z_copy(a, ch, p):
        span = pl.ds(p * half, half)
        target, _, _ = ends(a, ch)
        return remote(
            z_out.at[a, ch, span], z_in.at[line, span],
            zs.at[a, ch, p], zr.at[line, p], at(target, side, core),
        )

    def t_copy(a, ch, p):
        span = pl.ds(p * half, half)
        _, _, middle = ends(a, ch)
        return remote(
            z_out.at[a, ch, span], t_in.at[span], zs.at[a, ch, p], tr.at[p], at(middle, side, core)
        )

    def joined(a, ch, p):
        span = slice(p * half, (p + 1) * half)
        return c_sum[2 * a + 1, ch, span].astype(F32) + x_buf[a, ch, span].astype(F32)

    def join_sides(a, ch, p):
        span = slice(p * half, (p + 1) * half)
        target, leaf, middle = ends(a, ch)
        x_copy(a, ch, p).wait_recv()

        @pl.when(line == target)
        def _():
            gw_ref[span, :] = joined(a, ch, p)

        plain = line != target
        if leaf is not None:
            plain = plain & (line != leaf) & (line != middle)

            @pl.when(line == leaf)
            def _():
                z_out[a, ch, span] = joined(a, ch, p).astype(BF16)
                t_copy(a, ch, p).start()

        @pl.when(plain)
        def _():
            z_out[a, ch, span] = joined(a, ch, p).astype(BF16)
            z_copy(a, ch, p).start()

    def join_lines(a, ch, p):
        span = slice(p * half, (p + 1) * half)
        _, leaf, middle = ends(a, ch)
        if leaf is None:
            return

        @pl.when(line == middle)
        def _():
            t_copy(a, ch, p).wait_recv()
            z_out[a, ch, span] = (joined(a, ch, p) + t_in[span].astype(F32)).astype(BF16)
            z_copy(a, ch, p).start()

    def input_rows(j):
        span = tok_count // 4
        sl = slice(j * span, (j + 1) * span)
        git_ref[:, sl] = dot(gkv[:, sl], w_ref[...], ((0,), (0,))).astype(BF16).T

    loads[0].wait()
    for p in range(2):
        for d in (1, -1):

            @pl.when(inside(d))
            def _():
                gz_copy(d, 0, p).start()

        gx_copy(0, p).start()
    for p in range(2):
        c_near(0, p).start()
    for p in range(2):
        piece(0, side, p)[...] = own_ref[p * half:(p + 1) * half, :]

    @pl.when(jnp.logical_not(has_prev))
    def _():
        kv_ref[:, :WINDOW] = jnp.zeros((kv_ref.shape[0], WINDOW), BF16)

    loads[1].wait()
    for k in range(tok_count // WINDOW):
        x_ref[k * WINDOW:(k + 1) * WINDOW, :] = xt_ref[:, k * WINDOW:(k + 1) * WINDOW].T
    steps = [[0]] + [[2 * s - 1, 2 * s] for s in range(1, lines)]
    for s in range(1, lines + 2):
        for stage, lag in ((land, 0), (cross, 1), (project, 2)):
            if 0 <= s - lag < lines:
                for j in steps[s - lag]:
                    stage(j)

    for load in loads[2:]:
        load.wait()
    band(0, 1)
    band(0, 2)
    wait_kv_halo(0)
    wait_kv_halo(2)
    band(1, 0)
    send_halo(1)
    band(0, 0)
    send_halo(0)
    for t in range(3, tiles):
        band(0, t)
    wait_kv_halo(1)
    wait_kv_halo(3)
    band(2, 0)
    send_halo(2)
    finish(0)
    band(3, 0)
    send_halo(3)
    join(0)
    for t in range(1, tiles):
        band(1, t)
    finish(1)
    band(2, 1)
    join(1)
    join_sides(0, *early[0])
    band(2, 2)
    join_sides(0, *early[1])
    for t in range(3, tiles):
        band(2, t)
    finish(2)
    join_sides(0, *early[2])
    join_lines(0, *quarters[0])
    band(3, 1)
    join(2)
    join_sides(0, *early[3])
    band(3, 2)
    join_lines(0, *quarters[1])
    band(3, 3)
    for t in range(4, tiles):
        band(3, t)
    finish(3)
    input_rows(0)
    join(3)
    for i, q in enumerate(later):
        join_sides(1, *q)
        if i < 3:
            input_rows(i + 1)
        if i:
            join_lines(1, *later[i - 1])
    join_lines(1, *later[3])

    for a in range(2):
        for ch in range(2):
            target, leaf, middle = ends(a, ch)

            @pl.when(line == target)
            def _():
                for source in range(lines):
                    if source not in (target, leaf):
                        for p in range(2):
                            span = slice(p * half, (p + 1) * half)
                            remote(
                                z_out.at[a, ch, pl.ds(p * half, half)],
                                z_in.at[source, pl.ds(p * half, half)],
                                zs.at[a, ch, p], zr.at[source, p], at(source, side, core),
                            ).wait_recv()
                            gw_ref[span, :] += z_in[source, span].astype(F32)

    for k in range(4):
        c_copy(k).wait_send()

        @pl.when(has_prev)
        def _():
            halo(k).wait_send()

    for a in range(2):
        for ch, p in quarters:
            x_copy(a, ch, p).wait_send()

            @pl.when(line != a + 2 * ch)
            def _():
                z_copy(a, ch, p).wait_send()

    for j, (d, s) in enumerate(slots):

        @pl.when(valid(j))
        def _():
            for p in range(2):
                if s + 1 < lines:
                    for d_ in (1, -1) if s == 0 else (d,):

                        @pl.when(inside(d_))
                        def _():
                            gz_copy(d_, s, p).wait_send()

                gx_copy(j, p).wait_send()
                c_near(j, p).wait_send()
                c_far(j, p).wait_send()

    for line_ in range(lines):

        @pl.when(has_next)
        def _():
            kv_halo(line_).wait_send()


def fused(sink_logits, queries, out_grad, inputs_t, kv_weight, count):
    lines = count // 4
    depth, tok_count = inputs_t.shape
    rows = kv_weight.shape[0]
    width = rows * count
    slots = len(line_slots(lines))
    dma = pltpu.SemaphoreType.DMA
    vmem = pl.BlockSpec(memory_space=pltpu.VMEM)
    hbm = pl.BlockSpec(memory_space=pltpu.HBM)

    def low(*shape):
        return pltpu.VMEM(shape, BF16)

    operands = [
        pltpu.with_memory_space_constraint(a, pltpu.HBM)
        for a in (sink_logits, queries, out_grad, inputs_t, kv_weight)
    ]
    return pl.pallas_call(
        fused_kernel,
        in_specs=[hbm] * 5,
        out_specs=(vmem, vmem, vmem),
        out_shape=(
            jax.ShapeDtypeStruct(queries.shape, BF16),
            jax.ShapeDtypeStruct((depth, tok_count), BF16),
            jax.ShapeDtypeStruct((rows, depth), F32),
        ),
        scratch_shapes=[
            pltpu.SMEM(sink_logits.shape, F32),
            low(*queries.shape),
            low(*queries.shape),
            low(depth, tok_count),
            low(tok_count, depth),
            low(rows, depth),
            low(width, depth),
            low(width, WINDOW + tok_count),
            pltpu.VMEM((KV_HEADS, 2 * HEAD_DIM, WINDOW + tok_count), F32),
            low(width, tok_count),
            low(KV_HEADS, 2 * HEAD_DIM, WINDOW),
            low(KV_HEADS, 2 * HEAD_DIM, WINDOW),
            low(4, 2, 2, rows, depth),
            low(4, 2, rows, depth),
            low(4, 2, rows, depth),
            low(2, 2, rows, depth),
            low(2, 2, rows, depth),
            low(lines, rows, depth),
            low(rows, depth),
            dma((5,)), dma((2, lines - 1, 2)), dma((2, lines - 1, 2)),
            dma((slots, 2)), dma((slots, 2)), dma((slots, 2, 2)), dma((slots, 2, 2)),
            dma((lines,)), dma((lines,)),
            dma((4,)), dma((4,)), dma((4,)), dma((4,)), dma((2, 2, 2)), dma((2, 2, 2)),
            dma((2, 2, 2)), dma((lines, 2)), dma((2,)),
        ],
        compiler_params=pltpu.CompilerParams(
            collective_id=0, has_side_effects=True, vmem_limit_bytes=48 << 20
        ),
        name="fused",
    )(*operands)


def store_kernel(dq_ref, git_ref, gw_ref, dq_hbm, git_hbm, gw_hbm, sems):
    copies = []
    for src, dst, cuts in ((git_ref, git_hbm, 3), (dq_ref, dq_hbm, 2), (gw_ref, gw_hbm, 1)):
        step = src.shape[0] // cuts
        for i in range(cuts):
            span = pl.ds(i * step, step)
            copies.append(pltpu.make_async_copy(src.at[span], dst.at[span], sems.at[len(copies)]))
    for copy in copies:
        copy.start()
    for copy in copies:
        copy.wait()


def store(*arrays):
    return pl.pallas_call(
        store_kernel,
        in_specs=[pl.BlockSpec(memory_space=pltpu.VMEM)] * 3,
        out_specs=[pl.BlockSpec(memory_space=pltpu.HBM)] * 3,
        out_shape=[jax.ShapeDtypeStruct(a.shape, a.dtype) for a in arrays],
        scratch_shapes=[pltpu.SemaphoreType.DMA((10,))],
        compiler_params=pltpu.CompilerParams(vmem_limit_bytes=8 << 20),
        name="store",
    )(*arrays)


def shards(inputs, queries, out_grad, kv_weight, sink_logits):
    index = lax.axis_index("ctx")
    count = lax.axis_size("ctx")
    rows = 2 * KV_WIDTH // count
    direct = count == 16 and kv_weight.shape[0] == rows and inputs.shape[0] % (4 * WINDOW) == 0
    if direct:
        inputs_t = inputs.T
        grad_queries, grad_input_t, grad_weight = fused(
            sink_logits, queries, out_grad, inputs_t, kv_weight, count
        )
        grad_queries, grad_input_t, grad_weight = store(grad_queries, grad_input_t, grad_weight)
        return (grad_queries, grad_input_t.T, grad_weight)
    full_weight = lax.all_gather(kv_weight, "ctx", axis=0, tiled=True)
    kv_rows = dot(inputs, full_weight, ((1,), (1,))).astype(BF16)
    kv_prev = shifted(kv_rows[-WINDOW:], "ctx", 1)
    kv_ext = jnp.concatenate([kv_prev, kv_rows], axis=0)
    sink_rows = jnp.repeat(sink_logits.reshape(KV_HEADS, GROUP), WINDOW, axis=1)
    grad_queries, grad_ext = band_grads(
        index.astype(jnp.int32).reshape(1), sink_rows, queries, out_grad, kv_ext
    )
    back = shifted(grad_ext[:WINDOW].astype(BF16), "ctx", -1).astype(F32)
    own = grad_ext[WINDOW:]
    grad_kv = jnp.concatenate([own[:-WINDOW], own[-WINDOW:] + back], axis=0).astype(BF16)
    partial = dot(grad_kv, inputs, ((0,), (0,))).astype(BF16)
    grad_weight = lax.psum_scatter(partial, "ctx", scatter_dimension=0, tiled=True).astype(F32)
    grad_input = dot(grad_kv, full_weight, ((1,), (0,))).astype(BF16)
    return (grad_queries, grad_input, grad_weight)


def solution(mesh):
    placed = P(("rep", "ctx"), None)
    return jax.shard_map(
        shards,
        mesh=mesh,
        in_specs=(placed, placed, placed, placed, P()),
        out_specs=(placed, placed, placed),
        check_vma=False,
    )
```
